256 devices in a mesh: row: 64 (over z, y, core), col: 4 (over x).
Axes of the slice: x: 4, y: 4, z: 8, core: 2. Of those that a mesh axis runs over, the one named last changes fastest.
Arguments:
- sigma_anc: float32 [8192, 8192], P('row', 'col'), may hold values from -24 to 80, as said below
- panel_hat: float32 [8192, 4096], P('row', 'col'), may hold values from -0.0625 to 0.0625
- pattern: int32 [64, 64], replicated, may hold values from 0 to 1, as said below
- diag_inverse: float32 [4096], P('col'), may hold values from 0.5 to 4
Outputs:
- sigma_cross: float32 [8192, 4096], P('row', 'col')
- variance: float32 [4096], P('col')
The draws below stay inside these ranges and needn't reach their ends.
Inputs may be any that keep to these rules, and one draw needn't show every extreme that they name: `pattern`: symmetric; every diagonal block is 1. `sigma_anc`: symmetric.
All inputs are finite; a program needn't handle non-finite values.
Results may differ from the reference program's by a relative error of at most 0.000073.
Values sent between devices are 32-bit elements; how exact they have to be, the bound alone decides.
A program may use at most 128 MiB of HBM per device.

```python
import math
import jax
import jax.numpy as jnp
from jax import lax

WIDTH = 4096
BLOCK = 128
ANC = 8192


def draw_sigma_anc(key, part):
    normals = jax.random.normal(key, (ANC, ANC), jnp.float32)
    jitter = jnp.clip((normals + normals.T) * (0.5 / math.sqrt(2.0)), -1.5, 1.5)
    positions = lax.iota(jnp.float32, ANC)
    length = max(ANC / 8.0, 1.0)
    distance = jnp.abs(positions[:, None] - positions[None, :])
    smooth = jnp.exp(-distance / length)
    matrix = jitter + 0.5 * smooth + 2.0 * jnp.eye(ANC, dtype=jnp.float32)
    return matrix


def draw_pattern(key, part):
    blocks = ANC // BLOCK
    indices = lax.iota(jnp.int32, blocks)
    further = jnp.maximum(indices[:, None], indices[None, :])
    cutoff = 16 + 48 * further // blocks
    draws = jax.random.randint(key, (blocks, blocks), 0, 64)
    upper_half = (draws < cutoff) & (indices[:, None] <= indices[None, :])
    symmetric = upper_half | upper_half.T | (indices[:, None] == indices[None, :])
    return symmetric.astype(jnp.int32)


def block_scale(rng, shape, shards, least, largest):
    def one(axis_at, blocks):
        heights = jax.random.uniform(jax.random.fold_in(jax.random.fold_in(rng, 6), axis_at), (blocks,), jnp.float32, least / len(shards), largest / len(shards))
        return jnp.repeat(jnp.exp(heights), shape[axis_at] // blocks).reshape((-1,) + (1,) * (len(shape) - axis_at - 1))

    gain = one(*shards[0])
    for cut in shards[1:]:
        gain = gain * one(*cut)
    return gain


def scatter_about(own_key, dims, spread, limit, shards=(), kind=jnp.bfloat16):
    array = jax.random.normal(own_key, dims, jnp.float32) * spread
    if len(shards) > 0:
        array = block_scale(own_key, dims, shards, -0.22, 0.18) * array
    return jnp.clip(array, min=-limit, max=limit).astype(kind)


def setup_inputs(seed: int = 0) -> dict:
    arg_keys = jax.random.split(jax.random.key(seed), 5)
    return {
        "sigma_anc": draw_sigma_anc(jax.random.fold_in(arg_keys[4], 71), 0),
        "panel_hat": scatter_about(arg_keys[1], (ANC, WIDTH), ANC ** -0.5, 0.0625, ((0, 64), (1, 4)), jnp.float32),
        "pattern": draw_pattern(jax.random.fold_in(arg_keys[4], 71), 0),
        "diag_inverse": jnp.clip(jnp.exp(math.log(4.0) - 2.0794415 * jax.random.uniform(arg_keys[3], (WIDTH,), jnp.float32) ** block_scale(arg_keys[3], (WIDTH,), ((0, 4),), -0.2, 0.2)), 0.5, 4.0),
    }


def reference(sigma_anc, panel_hat, pattern, diag_inverse):
    blocks = pattern.shape[0]
    block_width = sigma_anc.shape[0] // blocks
    block_mask = pattern.astype(sigma_anc.dtype)
    block_mask = jnp.repeat(jnp.repeat(block_mask, block_width, axis=0), block_width, axis=1)
    masked = sigma_anc * block_mask
    sigma_cross = -jnp.dot(masked, panel_hat, precision=lax.Precision.HIGHEST, preferred_element_type=sigma_anc.dtype)
    variance = diag_inverse - jnp.sum(panel_hat * sigma_cross, axis=0)
    return sigma_cross, variance
```

```python
import functools
import heapq

import jax
import jax.numpy as jnp
from jax import lax
from jax.experimental import pallas as pl
from jax.experimental.pallas import tpu as pltpu
from jax.sharding import PartitionSpec as P

MESH = pl.DeviceIdType.MESH
NX, NY, NZ = 4, 4, 8
B = 128
W = 256
NS = 4
F32, BF16 = jnp.float32, jnp.bfloat16

LINK, LAT, CORE, CORE_LAT = 2.82, 1.8, 0.3, 1.0
T_ISSUE, T_PREP, T_TASK, T_SMALL = 0.06, 0.12, 1.2, 0.15


def hops(n, s):
    return 4 if (n % 2 == 0) == (s > 0) else 3


def plan():
    program, arrivals, free, done_at = [], [], {}, {}
    clock = [0.0]
    got, seq = set(), [0]

    def send(key, link, units=1.0):
        program.append(("send",) + key)
        clock[0] += T_ISSUE
        cost, lat = (CORE, CORE_LAT) if link == "c" else (LINK, LAT)
        start = max(clock[0], free.get(link, 0.0))
        free[link] = start + cost * units
        done_at[key] = free[link]
        seq[0] += 1
        heapq.heappush(arrivals, (free[link] + lat, seq[0], key))

    def sgn(s):
        return "+" if s > 0 else "-"

    def on(key):
        kind = key[0]
        if kind == "PZ":
            _, n, s, h = key
            if h < hops(n, s):
                send(("PZ", n, s, h + 1), "z" + sgn(s))
            send(("PC", n, (-s * h) % NZ), "c")
            if h == 2 and n + 2 < NS:
                send(("PZ", n + 2, s, 1), "z" + sgn(s))
                if s > 0:
                    send(("PC", n + 2, 0), "c")
        elif kind == "AR1":
            k = key[1]
            send(("AR2", k), "y" + "+-"[k])
        elif kind in ("AY", "AR2"):
            d, zz = ((-key[1]) % NY, key[2]) if kind == "AY" else (2, key[1])
            for s in (1, -1):
                send(("XS", d, zz, s, 1), "x" + sgn(s))
            got.add(("own", d, zz))
            if all(("own", e, f) in got for e in (1, 2, 3) for f in (0, 1)):
                for s in (1, -1):
                    send(("XS", 0, 1, s, 1), "x" + sgn(s))
        elif kind == "XS":
            _, d, zz, s, h = key
            if h == 1 and (zz == 0) == (s > 0):
                send(("XS", d, zz, s, 2), "x" + sgn(s))

    for s in (1, -1):
        send(("PZ", 0, s, 1), "z" + sgn(s))
        send(("AR1", 0 if s > 0 else 1), "y" + sgn(s))
        send(("XS", 0, 0, s, 1), "x" + sgn(s))
    send(("PC", 0, 0), "c")
    for s in (1, -1):
        send(("PZ", 1, s, 1), "z" + sgn(s))
        for zz in (0, 1):
            send(("AY", s, zz), "y" + sgn(s))
    send(("PC", 1, 0), "c")
    program.append(("local",))

    jobs = {}
    panel = {n: {("PZ", n, s, h) for s in (1, -1) for h in range(1, hops(n, s) + 1)} | {("PC", n, r) for r in range(NZ)} for n in range(NS)}
    rows = {}
    for d in range(NY):
        need = {("XS", d, zz, s, 1) for zz in (0, 1) for s in (1, -1)} | {("XS", d, 0, 1, 2), ("XS", d, 1, -1, 2)}
        need |= {0: set(), 2: {("AR2", 0), ("AR2", 1)}}.get(d, {("AY", 1 if d == 3 else -1, 0), ("AY", 1 if d == 3 else -1, 1)})
        rows[d] = need
    order = {2: 0, 1: 1, 3: 2, 0: 3}
    for d in range(NY):
        jobs[("prepA", d)] = (-1.0, rows[d], T_PREP * 8)
    for n in range(NS):
        jobs[("prepB", n)] = (-2.0, panel[n], T_PREP * 16)
        for d in range(NY):
            jobs[("task", d, n)] = (n + 0.1 * order[d], {("prepA", d), ("prepB", n)}, T_TASK)
        jobs[("y2", n)] = (-3.0, {("task", 2, n)}, 0.0)
        jobs[("y1", n, 1)] = (-3.0, {("task", 1, n), ("Y2", n, 1)}, T_SMALL)
        jobs[("y1", n, -1)] = (-3.0, {("task", 3, n), ("Y2", n, -1)}, T_SMALL)
        jobs[("fin", n)] = (-3.0, {("task", 0, n), ("Y1", n, 1), ("Y1", n, -1)}, T_SMALL)
    while jobs or arrivals:
        if arrivals and arrivals[0][0] <= clock[0]:
            key = heapq.heappop(arrivals)[2]
            program.append(("recv",) + key)
            clock[0] += T_ISSUE
            got.add(key)
            on(key)
            continue
        ready = [(p, j) for j, (p, need, _) in jobs.items() if need <= got]
        if ready:
            job = min(ready, key=lambda r: (r[0], str(r[1])))[1]
            program.append(job)
            clock[0] += jobs.pop(job)[2]
            got.add(job)
            if job[0] == "y2":
                for s in (1, -1):
                    send(("Y2", job[1], s), "y" + sgn(s), 0.5)
            elif job[0] == "y1":
                send(("Y1", job[1], job[2]), "y" + sgn(job[2]))
            continue
        late = sorted((t, k) for k, t in done_at.items() if t + 1.0 < clock[0])
        if late and arrivals and arrivals[0][0] > clock[0] + 0.05:
            program.append(("sent",) + late[0][1])
            del done_at[late[0][1]]
            clock[0] += 0.03
            continue
        clock[0] = max(clock[0], arrivals[0][0])
    for key in sorted(done_at, key=done_at.get):
        program.append(("sent",) + key)
    return program, clock[0]


def kernel(program, sem_of, pattern, sigma, panel, diag, cross, var, pbuf, sbuf, relay, a_hi, a_lo, b_hi, b_lo, part, r1, r2,
           va, vb, send_sem, recv_sem, va_send, va_recv, vb_send, vb_recv, local_sem):
    row, x = lax.axis_index("row"), lax.axis_index("col")
    z, y, c = row // (2 * NY), (row // 2) % NY, row % 2

    def at(dx=0, dy=0, dz=0, flip=False):
        core = 1 - c if flip else c
        return ((((z + dz + NZ) % NZ) * NY + (y + dy + NY) % NY) * 2 + core, (x + dx + NX) % NX)

    def lanes(start):
        return pl.ds(pl.multiple_of(start, W), W)

    def ends(key, sender):
        kind = key[0]
        if kind == "PZ":
            _, n, s, h = key
            zs = (z - s * (h - 1 if sender else h) + NZ) % NZ
            dst = pbuf.at[n, 2 * zs + c]
            src = panel.at[:, pl.ds(n * W, W)] if h == 1 else dst
            return src, dst, at(dz=s)
        if kind == "PC":
            _, n, rel = key
            zs = (z + rel) % NZ
            dst = pbuf.at[n, 2 * zs + (c if sender else 1 - c)]
            src = panel.at[:, pl.ds(n * W, W)] if rel == 0 else dst
            return src, dst, at(flip=True)
        if kind == "AY":
            _, s, zz = key
            src = sigma.at[:, lanes(zz * NY * W + ((y + s + NY) % NY) * W)]
            return src, sbuf.at[(-s) % NY, 2 * x + zz], at(dy=s)
        if kind == "AR1":
            k = key[1]
            src = sigma.at[:, lanes(k * NY * W + ((y + 2) % NY) * W)]
            return src, relay.at[k], at(dy=1 - 2 * k)
        if kind == "AR2":
            k = key[1]
            return relay.at[k], sbuf.at[2, 2 * x + k], at(dy=1 - 2 * k)
        if kind == "XS":
            _, d, zz, s, h = key
            xs = (x - s * (h - 1 if sender else h) + NX) % NX
            dst = sbuf.at[d, 2 * xs + zz]
            src = sigma.at[:, lanes(zz * NY * W + y * W)] if d == 0 and h == 1 else dst
            return src, dst, at(dx=s)
        if kind == "Y2":
            _, n, s = key
            i = 0 if s > 0 else 1
            return part.at[2, n, pl.ds(i * (B // 2), B // 2)], r1.at[i, n], at(dy=s)
        _, n, s = key
        return part.at[s % NY, n], r2.at[0 if s > 0 else 1, n], at(dy=s)

    def copy(key, sender):
        src, dst, target = ends(key, sender)
        i = sem_of[key]
        return pltpu.make_async_remote_copy(
            src_ref=src if sender else dst, dst_ref=dst, send_sem=send_sem.at[i], recv_sem=recv_sem.at[i], device_id=target,
            device_id_type=MESH)

    barrier = pltpu.get_barrier_semaphore()
    me8 = row % (2 * NY)
    group = [(z * 2 * NY + (me8 + r) % (2 * NY), x) for r in range(1, 2 * NY)]
    stack = [at(dz=r) for r in range(1, NZ)]
    peers = group + stack + [at(dx=1), at(dx=-1)]
    for peer in peers:
        pl.semaphore_signal(barrier, inc=1, device_id=peer, device_id_type=MESH)
    pl.semaphore_wait(barrier, len(peers))

    locals_ = [pltpu.make_async_copy(panel.at[:, pl.ds(n * W, W)], pbuf.at[n, 2 * z + c], local_sem.at[n]) for n in range(NS)]
    locals_ += [pltpu.make_async_copy(sigma.at[:, lanes(zz * NY * W + y * W)], sbuf.at[0, 2 * x + zz], local_sem.at[NS + zz]) for zz in (0, 1)]

    def prep_a(d):
        if d == 0:
            for zz in (0, 1):
                locals_[NS + zz].wait()
        rb = (z * NY + (y + d) % NY) * 2 + c

        def one(zk, carry):
            cb = (zk * NY + y) * 2
            for j in (0, 1):
                m = pattern[rb, cb + j].astype(F32)
                s = sbuf[d, zk, :, pl.ds(j * B, B)] * m
                hi = s.astype(BF16)
                a_hi[zk, pl.ds(d * B, B), pl.ds(j * B, B)] = hi
                a_lo[zk, pl.ds(d * B, B), pl.ds(j * B, B)] = (s - hi.astype(F32)).astype(BF16)
            return carry

        lax.fori_loop(0, NZ, one, 0)

    def prep_b(n):
        locals_[n].wait()

        def one(k, carry):
            for j in (0, 1):
                p = pbuf[n, 2 * k + j]
                hi = p.astype(BF16)
                b_hi[n, k, pl.ds(j * B, B)] = hi
                b_lo[n, k, pl.ds(j * B, B)] = (p - hi.astype(F32)).astype(BF16)
            return carry

        lax.fori_loop(0, NZ, one, 0)

    def task(d, n):
        def one(k, acc):
            hi, lo = a_hi[k, pl.ds(d * B, B)], a_lo[k, pl.ds(d * B, B)]
            dot = functools.partial(jnp.dot, preferred_element_type=F32)
            return acc + (dot(hi, b_hi[n, k]) + (dot(hi, b_lo[n, k]) + dot(lo, b_hi[n, k])))

        part[d, n] = lax.fori_loop(0, NZ, one, jnp.zeros((B, W), F32))

    for act in program:
        kind = act[0]
        if kind == "send":
            copy(act[1:], True).start()
        elif kind == "recv":
            copy(act[1:], False).wait_recv()
        elif kind == "sent":
            copy(act[1:], True).wait_send()
        elif kind == "local":
            for cp in locals_:
                cp.start()
        elif kind == "prepA":
            prep_a(act[1])
        elif kind == "prepB":
            prep_b(act[1])
        elif kind == "task":
            task(act[1], act[2])
        elif kind == "y1":
            _, n, s = act
            i = 0 if s > 0 else 1
            half = pl.ds(i * (B // 2), B // 2)
            part[s % NY, n, half] = part[s % NY, n, half] + r1[i, n]
        elif kind == "fin":
            n = act[1]
            out = -(part[0, n] + (r2[0, n] + r2[1, n]))
            cross[:, pl.ds(n * W, W)] = out
            prod = jnp.sum(out * pbuf[n, 2 * z + c], axis=0, keepdims=True)
            for j in (0, 1):
                va[me8, pl.ds(2 * n + j, 1)] = prod[:, j * B:(j + 1) * B]

    def exchange(buf, mine, members, n, ssem, rsem, base):
        cps = []
        for r in range(1, n):
            cps.append(pltpu.make_async_remote_copy(
                src_ref=buf.at[mine], dst_ref=buf.at[mine], send_sem=ssem.at[r], recv_sem=rsem.at[r], device_id=members[r - 1],
                device_id_type=MESH))
            cps[-1].start()
        for r in range(1, n):
            slot = buf.at[(mine - r + n) % n]
            pltpu.make_async_remote_copy(
                src_ref=slot, dst_ref=slot, send_sem=ssem.at[r], recv_sem=rsem.at[r], device_id=members[r - 1],
                device_id_type=MESH).wait_recv()
        total = buf[0]
        for i in range(1, n):
            total = total + buf[i]
        return total, cps

    total, first = exchange(va, me8, group, 2 * NY, va_send, va_recv, 0)
    vb[z] = total
    total, second = exchange(vb, z, stack, NZ, vb_send, vb_recv, 0)
    var[...] = diag[...] - total
    for cp in first + second:
        cp.wait_send()


def body(sigma_anc, panel_hat, pattern, diag_inverse):
    program, _ = plan()
    keys = sorted({act[1:] for act in program if act[0] == "send"}, key=str)
    sem_of = {key: i for i, key in enumerate(keys)}
    dma = pltpu.SemaphoreType.DMA
    vmem = pl.BlockSpec(memory_space=pltpu.VMEM)
    anywhere = pl.BlockSpec(memory_space=pl.ANY)
    cross, var = pl.pallas_call(
        functools.partial(kernel, program, sem_of),
        out_shape=(jax.ShapeDtypeStruct((B, NS * W), F32), jax.ShapeDtypeStruct((8, B), F32)),
        in_specs=[pl.BlockSpec(memory_space=pltpu.SMEM), anywhere, anywhere, vmem],
        out_specs=(vmem, vmem),
        scratch_shapes=[
            pltpu.VMEM((NS, 2 * NZ, B, W), F32),
            pltpu.VMEM((NY, NZ, B, W), F32),
            pltpu.VMEM((2, B, W), F32),
            pltpu.VMEM((NZ, NY * B, W), BF16),
            pltpu.VMEM((NZ, NY * B, W), BF16),
            pltpu.VMEM((NS, NZ, W, W), BF16),
            pltpu.VMEM((NS, NZ, W, W), BF16),
            pltpu.VMEM((NY, NS, B, W), F32),
            pltpu.VMEM((2, NS, B // 2, W), F32),
            pltpu.VMEM((2, NS, B, W), F32),
            pltpu.VMEM((2 * NY, 8, B), F32),
            pltpu.VMEM((NZ, 8, B), F32),
            dma((len(keys),)),
            dma((len(keys),)),
            dma((2 * NY,)),
            dma((2 * NY,)),
            dma((NZ,)),
            dma((NZ,)),
            dma((NS + 2,)),
        ],
        compiler_params=pltpu.CompilerParams(collective_id=0, has_side_effects=True, vmem_limit_bytes=56 * 1024 * 1024),
        name="selected_inverse",
    )(pattern, sigma_anc, panel_hat, diag_inverse.reshape(8, B))
    return cross, var.reshape(-1)


def solution(mesh):
    in_specs = (P("row", "col"), P("row", "col"), P(), P("col"))
    out_specs = (P("row", "col"), P("col"))
    return jax.shard_map(body, mesh=mesh, in_specs=in_specs, out_specs=out_specs, check_vma=False)
```

```python
import functools
import heapq

import jax
import jax.numpy as jnp
from jax import lax
from jax.experimental import pallas as pl
from jax.experimental.pallas import tpu as pltpu
from jax.sharding import PartitionSpec as P

MESH = pl.DeviceIdType.MESH
NX, NY, NZ = 4, 4, 8
B = 128
W = 256
NS = 4
F32, BF16 = jnp.float32, jnp.bfloat16

LINK, LAT, CORE, CORE_LAT = 2.82, 1.8, 0.3, 1.0
T_ISSUE, T_PREP, T_TASK, T_SMALL, T_STEP = 0.03, 0.035, 0.96, 0.1, 0.45
LAST = NS - 1
VA_LAT, VB_LAT = 2.6, 4.2


def hops(n, s):
    return 4 if (n % 2 == 0) == (s > 0) else 3


def plan():
    program, arrivals, free, done_at = [], [], {}, {}
    clock = [0.0]
    got, seq = set(), [0]

    def send(key, link, units=1.0):
        program.append(("send",) + key)
        clock[0] += T_ISSUE
        cost, lat = {"c": (CORE, CORE_LAT), "va": (0.0, VA_LAT), "vb": (0.0, VB_LAT)}.get(link, (LINK, LAT))
        start = max(clock[0], free.get(link, 0.0))
        free[link] = start + cost * units
        done_at[key] = free[link]
        seq[0] += 1
        heapq.heappush(arrivals, (free[link] + lat, seq[0], key))

    def sgn(s):
        return "+" if s > 0 else "-"

    def on(key):
        kind = key[0]
        if kind == "PZ":
            _, n, s, h = key
            if h < hops(n, s):
                send(("PZ", n, s, h + 1), "z" + sgn(s))
            send(("PC", n, (-s * h) % NZ), "c")
            if h == 2 and n + 2 < NS:
                send(("PZ", n + 2, s, 1), "z" + sgn(s))
                if s > 0:
                    send(("PC", n + 2, 0), "c")
        elif kind == "AR1":
            k = key[1]
            send(("AR2", k), "y" + "+-"[k])
            send(("AY", 1 - 2 * k, 1), "y" + "+-"[k])
            send(("PY", 1 - 2 * k, 1), "y" + "+-"[k])
        elif kind == "PY" and key[2] == 1:
            send(("PY", key[1], 2), "y" + sgn(key[1]), 0.5)
        elif kind in ("AY", "AR2"):
            d, zz = ((-key[1]) % NY, key[2]) if kind == "AY" else (2, key[1])
            for s in (1, -1):
                send(("XS", d, zz, s, 1), "x" + sgn(s))
        elif kind == "XS":
            _, d, zz, s, h = key
            if h == 1 and (zz == 0) == (s > 0):
                send(("XS", d, zz, s, 2), "x" + sgn(s))

    for s in (1, -1):
        send(("PZ", 0, s, 1), "z" + sgn(s))
        send(("AR1", 0 if s > 0 else 1), "y" + sgn(s))
        send(("XS", 0, 0, s, 1), "x" + sgn(s))
    send(("PC", 0, 0), "c")
    for s in (1, -1):
        send(("XS", 0, 1, s, 1), "x" + sgn(s))
        send(("PZ", 1, s, 1), "z" + sgn(s))
        send(("AY", s, 0), "y" + sgn(s))
    send(("PC", 1, 0), "c")
    program.append(("local",))

    jobs = {}
    panel = {n: {("PZ", n, s, h) for s in (1, -1) for h in range(1, hops(n, s) + 1)} | {("PC", n, r) for r in range(NZ)} for n in range(NS)}
    rows = {}
    for d in range(NY):
        need = {("XS", d, zz, s, 1) for zz in (0, 1) for s in (1, -1)} | {("XS", d, 0, 1, 2), ("XS", d, 1, -1, 2)}
        need |= {0: set(), 2: {("AR2", 0), ("AR2", 1)}}.get(d, {("AY", 1 if d == 3 else -1, 0), ("AY", 1 if d == 3 else -1, 1)})
        rows[d] = need
    order = {2: 0, 1: 1, 3: 2, 0: 3}
    for d in range(NY):
        jobs[("prepA", d)] = (-1.0, rows[d], T_PREP * 8)
    for rel in range(NZ):
        units = {("PC", LAST, rel)}
        if rel:
            units |= {("PZ", LAST, s, h) for s in (1, -1) for h in range(1, hops(LAST, s) + 1) if (-s * h) % NZ == rel}
        jobs[("step", rel)] = (LAST - 0.5, {("prepA", d) for d in range(NY)} | units | ({("step", 0)} if rel else set()), T_STEP)
    jobs[("vlast",)] = (-4.0, {("step", rel) for rel in range(NZ)} | {("PY", s, h) for s in (1, -1) for h in (1, 2)} | {("fin", n) for n in range(LAST)}, 0.5)
    jobs[("vsum",)] = (-4.0, {("VA", r) for r in range(1, 2 * NY)}, 0.05)
    jobs[("vend",)] = (-4.0, {("VB", r) for r in range(1, NZ)}, 0.05)
    for n in range(NS):
        if n < LAST:
            jobs[("prepB", n)] = (-2.0, panel[n], T_PREP * 16)
            for d in range(NY):
                jobs[("task", d, n)] = (n + 0.1 * order[d], {("prepA", d), ("prepB", n)}, T_TASK)
        else:
            for d in range(NY):
                jobs[("task", d, n)] = (-3.5, {("vlast",)}, 0.0)
        jobs[("y2", n)] = (-3.0, {("task", 2, n)}, 0.0)
        jobs[("y1", n, 1)] = (-3.0, {("task", 1, n), ("Y2", n, 1)}, T_SMALL)
        jobs[("y1", n, -1)] = (-3.0, {("task", 3, n), ("Y2", n, -1)}, T_SMALL)
        jobs[("fin", n)] = (-3.0, {("task", 0, n), ("Y1", n, 1), ("Y1", n, -1)}, T_SMALL)
    while jobs or arrivals:
        if arrivals and arrivals[0][0] <= clock[0]:
            key = heapq.heappop(arrivals)[2]
            program.append(("recv",) + key)
            clock[0] += T_ISSUE
            got.add(key)
            on(key)
            continue
        ready = [(p, j) for j, (p, need, _) in jobs.items() if need <= got]
        if ready:
            job = min(ready, key=lambda r: (r[0], str(r[1])))[1]
            program.append(job)
            clock[0] += jobs.pop(job)[2]
            got.add(job)
            if job[0] == "y2":
                for s in (1, -1):
                    send(("Y2", job[1], s), "y" + sgn(s), 0.5)
            elif job[0] == "vlast":
                for r in range(1, 2 * NY):
                    send(("VA", r), "va")
            elif job[0] == "vsum":
                for r in range(1, NZ):
                    send(("VB", r), "vb")
            elif job[0] == "y1":
                send(("Y1", job[1], job[2]), "y" + sgn(job[2]))
            continue
        late = sorted((t, k) for k, t in done_at.items() if t + 3.0 < clock[0])
        if late and arrivals and arrivals[0][0] > clock[0] + 0.05:
            program.append(("sent",) + late[0][1])
            del done_at[late[0][1]]
            clock[0] += 0.03
            continue
        clock[0] = max(clock[0], arrivals[0][0])
    for key in sorted(done_at, key=done_at.get):
        program.append(("sent",) + key)
    return program, clock[0], free


def kernel(program, sem_of, pattern_hbm, sigma, panel, cross, var, pattern, pbuf, sbuf, relay, a_hi, a_lo, b_hi, b_lo, part, r1, r2,
           pv, obuf, va, vb, send_sem, recv_sem, local_sem, out_sem):
    row, x = lax.axis_index("row"), lax.axis_index("col")
    z, y, c = row // (2 * NY), (row // 2) % NY, row % 2

    def at(dx=0, dy=0, dz=0, flip=False):
        core = 1 - c if flip else c
        return ((((z + dz + NZ) % NZ) * NY + (y + dy + NY) % NY) * 2 + core, (x + dx + NX) % NX)

    def lanes(start):
        return pl.ds(pl.multiple_of(start, W), W)

    def ends(key, sender):
        kind = key[0]
        if kind == "PZ":
            _, n, s, h = key
            zs = (z - s * (h - 1 if sender else h) + NZ) % NZ
            dst = pbuf.at[n, 2 * zs + c]
            src = panel.at[:, pl.ds(n * W, W)] if h == 1 else dst
            return src, dst, at(dz=s)
        if kind == "PC":
            _, n, rel = key
            zs = (z + rel) % NZ
            dst = pbuf.at[n, 2 * zs + (c if sender else 1 - c)]
            src = panel.at[:, pl.ds(n * W, W)] if rel == 0 else dst
            return src, dst, at(flip=True)
        if kind == "AY":
            _, s, zz = key
            src = sigma.at[:, lanes(zz * NY * W + ((y + s + NY) % NY) * W)]
            return src, sbuf.at[(-s) % NY, 2 * x + zz], at(dy=s)
        if kind == "AR1":
            k = key[1]
            src = sigma.at[:, lanes(k * NY * W + ((y + 2) % NY) * W)]
            return src, relay.at[k], at(dy=1 - 2 * k)
        if kind == "AR2":
            k = key[1]
            return relay.at[k], sbuf.at[2, 2 * x + k], at(dy=1 - 2 * k)
        if kind == "XS":
            _, d, zz, s, h = key
            xs = (x - s * (h - 1 if sender else h) + NX) % NX
            dst = sbuf.at[d, 2 * xs + zz]
            src = sigma.at[:, lanes(zz * NY * W + y * W)] if d == 0 and h == 1 else dst
            return src, dst, at(dx=s)
        if kind == "PY":
            _, s, h = key
            if h == 1:
                return panel.at[:, pl.ds(LAST * W, W)], pv.at[(-s) % NY], at(dy=s)
            half = pl.ds((0 if s > 0 else 1) * (B // 2), B // 2)
            return pv.at[(-s) % NY, half], pv.at[2, half], at(dy=s)
        if kind == "VA":
            slot = va.at[me8 if sender else (me8 - key[1] + 2 * NY) % (2 * NY)]
            return slot, slot, (z * 2 * NY + (me8 + key[1]) % (2 * NY), x)
        if kind == "VB":
            slot = vb.at[z if sender else (z - key[1] + NZ) % NZ]
            return slot, slot, at(dz=key[1])
        if kind == "Y2":
            _, n, s = key
            i = 0 if s > 0 else 1
            return part.at[n, 2, pl.ds(i * (B // 2), B // 2)], r1.at[i, n], at(dy=s)
        _, n, s = key
        return part.at[n, s % NY], r2.at[0 if s > 0 else 1, n], at(dy=s)

    def copy(key, sender):
        src, dst, target = ends(key, sender)
        i = sem_of[key]
        return pltpu.make_async_remote_copy(
            src_ref=src if sender else dst, dst_ref=dst, send_sem=send_sem.at[i], recv_sem=recv_sem.at[i], device_id=target,
            device_id_type=MESH)

    me8 = row % (2 * NY)
    barrier = pltpu.get_barrier_semaphore()
    peers = [at(dx=1), at(dx=-1), at(dy=1), at(dy=-1), at(dz=1), at(dz=-1), at(flip=True)]
    for peer in peers:
        pl.semaphore_signal(barrier, inc=1, device_id=peer, device_id_type=MESH)
    locals_ = [pltpu.make_async_copy(panel.at[:, pl.ds(n * W, W)], pbuf.at[n, 2 * z + c], local_sem.at[n]) for n in range(NS)]
    locals_ += [pltpu.make_async_copy(sigma.at[:, lanes(zz * NY * W + y * W)], sbuf.at[0, 2 * x + zz], local_sem.at[NS + zz]) for zz in (0, 1)]
    locals_ += [pltpu.make_async_copy(pattern_hbm, pattern, local_sem.at[NS + 2])]
    pl.semaphore_wait(barrier, len(peers))

    def prep_a(d):
        rb = (z * NY + (y + d) % NY) * 2 + c

        def one(zk, carry):
            cb = (zk * NY + y) * 2
            for j in (0, 1):
                m = pattern[rb, cb + j].astype(F32)
                s = sbuf[d, zk, :, pl.ds(j * B, B)] * m
                hi = s.astype(BF16)
                a_hi[zk, pl.ds(d * B, B), pl.ds(j * B, B)] = hi
                a_lo[zk, pl.ds(d * B, B), pl.ds(j * B, B)] = (s - hi.astype(F32)).astype(BF16)
            return carry

        lax.fori_loop(0, NZ, one, 0)

    def split_b(n, k):
        for j in (0, 1):
            p = pbuf[n, 2 * k + j]
            hi = p.astype(BF16)
            b_hi[n, k, pl.ds(j * B, B)] = hi
            b_lo[n, k, pl.ds(j * B, B)] = (p - hi.astype(F32)).astype(BF16)

    def prep_b(n):
        def one(k, carry):
            split_b(n, k)
            return carry

        lax.fori_loop(0, NZ, one, 0)

    dot = functools.partial(jnp.dot, preferred_element_type=F32)

    def task(d, n):
        acc = jnp.zeros((B, W), F32)
        for k in range(NZ):
            hi, lo = a_hi[k, pl.ds(d * B, B)], a_lo[k, pl.ds(d * B, B)]
            acc = acc + (dot(hi, b_hi[n, k]) + (dot(hi, b_lo[n, k]) + dot(lo, b_hi[n, k])))
        part[n, d] = acc

    def step(rel):
        k = (z + rel) % NZ
        split_b(LAST, k)
        hi, lo = a_hi[k], a_lo[k]
        res = (dot(hi, b_hi[LAST, k]) + (dot(hi, b_lo[LAST, k]) + dot(lo, b_hi[LAST, k]))).reshape(NY, B, W)
        part[LAST] = part[LAST] + res if rel else res

    def put_var(n, prod):
        for j in (0, 1):
            va[me8, pl.ds(2 * n + j, 1)] = prod[:, j * B:(j + 1) * B]

    outs = [pltpu.make_async_copy(obuf.at[n], cross.at[:, pl.ds(n * W, W)], out_sem.at[n]) for n in range(NS)]

    for act in program:
        kind = act[0]
        if kind == "send":
            copy(act[1:], True).start()
        elif kind == "recv":
            copy(act[1:], False).wait_recv()
        elif kind == "sent":
            copy(act[1:], True).wait_send()
        elif kind == "local":
            for cp in locals_:
                cp.start()
            for cp in locals_:
                cp.wait()
        elif kind == "prepA":
            prep_a(act[1])
        elif kind == "prepB":
            prep_b(act[1])
        elif kind == "task":
            if act[2] < LAST:
                task(act[1], act[2])
        elif kind == "step":
            step(act[1])
        elif kind == "y1":
            _, n, s = act
            i = 0 if s > 0 else 1
            half = pl.ds(i * (B // 2), B // 2)
            part[n, s % NY, half] = part[n, s % NY, half] + r1[i, n]
        elif kind == "fin":
            n = act[1]
            out = part[n, 0] + (r2[0, n] + r2[1, n])
            obuf[n] = out
            outs[n].start()
            if n < LAST:
                put_var(n, jnp.sum(out * pbuf[n, 2 * z + c], axis=0, keepdims=True))
        elif kind == "vlast":
            prod = part[LAST, 0] * pbuf[LAST, 2 * z + c]
            for d in range(1, NY):
                prod = prod + part[LAST, d] * pv[d]
            put_var(LAST, jnp.sum(prod, axis=0, keepdims=True))
        elif kind == "vsum":
            total = va[0]
            for i in range(1, 2 * NY):
                total = total + va[i]
            vb[z] = total
        elif kind == "vend":
            total = vb[0]
            for i in range(1, NZ):
                total = total + vb[i]
            var[...] = total
    for cp in outs:
        cp.wait()


def body(sigma_anc, panel_hat, pattern, diag_inverse):
    program = plan()[0]
    keys = sorted({act[1:] for act in program if act[0] == "send"}, key=str)
    sem_of = {key: i for i, key in enumerate(keys)}
    dma = pltpu.SemaphoreType.DMA
    vmem = pl.BlockSpec(memory_space=pltpu.VMEM)
    anywhere = pl.BlockSpec(memory_space=pl.ANY)
    cross, var = pl.pallas_call(
        functools.partial(kernel, program, sem_of),
        out_shape=(pltpu.VMEM((B, NS * W), F32), pltpu.VMEM((8, B), F32)),
        in_specs=[pl.BlockSpec(memory_space=pltpu.HBM)] * 3,
        out_specs=(vmem, vmem),
        scratch_shapes=[
            pltpu.SMEM((NY * NZ * 2, NY * NZ * 2), jnp.int32),
            pltpu.VMEM((NS, 2 * NZ, B, W), F32),
            pltpu.VMEM((NY, NZ, B, W), F32),
            pltpu.VMEM((2, B, W), F32),
            pltpu.VMEM((NZ, NY * B, W), BF16),
            pltpu.VMEM((NZ, NY * B, W), BF16),
            pltpu.VMEM((NS, NZ, W, W), BF16),
            pltpu.VMEM((NS, NZ, W, W), BF16),
            pltpu.VMEM((NS, NY, B, W), F32),
            pltpu.VMEM((2, NS, B // 2, W), F32),
            pltpu.VMEM((2, NS, B, W), F32),
            pltpu.VMEM((NY, B, W), F32),
            pltpu.VMEM((NS, B, W), F32),
            pltpu.VMEM((2 * NY, 8, B), F32),
            pltpu.VMEM((NZ, 8, B), F32),
            dma((len(keys),)),
            dma((len(keys),)),
            dma((NS + 3,)),
            dma((NS,)),
        ],
        compiler_params=pltpu.CompilerParams(collective_id=0, has_side_effects=True, vmem_limit_bytes=56 * 1024 * 1024),
        name="selected_inverse",
    )(pattern, sigma_anc, panel_hat)
    return -cross, diag_inverse + var.reshape(-1)


def solution(mesh):
    in_specs = (P("row", "col"), P("row", "col"), P(), P("col"))
    out_specs = (P("row", "col"), P("col"))
    return jax.shard_map(body, mesh=mesh, in_specs=in_specs, out_specs=out_specs, check_vma=False)
```

```python
import functools
import heapq

import jax
import jax.numpy as jnp
from jax import lax
from jax.experimental import pallas as pl
from jax.experimental.pallas import tpu as pltpu
from jax.sharding import PartitionSpec as P

MESH = pl.DeviceIdType.MESH
NX, NY, NZ = 4, 4, 8
B = 128
W = 256
NS = 4
F32, BF16 = jnp.float32, jnp.bfloat16

EARLY = (2, 3)
STEPPED = (2, 3)
LATE_D = 1
POS = (0, 3, 1, 2)
FAR = NZ // 2
SEND_POOL = 40
Y_SHARED = 25.0
X_WINDOW = 2
NEXT = (None, (1, 2), (2, 3), (1, 2))

LINK, LAT, CORE, CORE_LAT = 2.82, 2.0, 0.3, 1.0
T_ISSUE, T_PREP, T_TASK, T_SMALL, T_STEP, T_BLOCK = 0.03, 0.035, 0.96, 0.1, 0.5, 0.4
VZ_LAT, VG_LAT = 4.2, 3.0
D_ORDER = (0, 2, 3, 1)


def subs(s, h):
    first = 0 if s > 0 else 1
    return (first,) if h == FAR else (first, 1 - first)


def sgn(s):
    return "+" if s > 0 else "-"


def plan():
    program, arrivals, free, done_at = [], [], {}, {}
    clock = [0.0]
    got, seq, ends = set(), [0], {}

    def send(key, link, units=1.0):
        program.append(("send",) + key)
        clock[0] += T_ISSUE
        cost, lat = {"c": (CORE, CORE_LAT), "vz": (0.0, VZ_LAT), "vg": (0.0, VG_LAT)}.get(link, (LINK, LAT))
        start = max(clock[0], free.get(link, 0.0))
        took = cost * units
        if link[0] == "y" and clock[0] > Y_SHARED:
            both = min(max(free.get("y+" if link == "y-" else "y-", 0.0) - start, 0.0), took)
            took = (took + both) / 2
        free[link] = start + took
        done_at[key] = ends[key] = free[link]
        seq[0] += 1
        heapq.heappush(arrivals, (free[link] + lat, seq[0], key))

    def pz(n, s, h, sub):
        send(("PZ", n, s, h, sub), "z" + sgn(s), 0.5)

    def start_slice(n, s):
        for sub in subs(s, 1):
            pz(n, s, 1, sub)

    order = {d: i for i, d in enumerate(D_ORDER)}
    held, under_way = [], {(0, 0): 2, (0, 1): 2}

    def forward_x():
        while held and len(under_way) < X_WINDOW:
            d, zz = min(held, key=lambda e: (order[e[0]], e[1]))
            if any(("own", e, f) not in got for e in D_ORDER[1:order[d]] for f in (0, 1)):
                return
            held.remove((d, zz))
            got.add(("own", d, zz))
            under_way[(d, zz)] = 2
            for s in (1, -1):
                send(("XS", d, zz, s, 1), "x" + sgn(s))

    def on(key):
        kind = key[0]
        if kind == "PZ":
            _, n, s, h, sub = key
            if h < FAR and sub in subs(s, h + 1):
                pz(n, s, h + 1, sub)
            if h == FAR:
                send(("PC", n, FAR, sub + 1), "c", 0.5)
            elif sub == subs(s, h)[1]:
                send(("PC", n, (-s * h) % NZ, 0), "c")
            for i, after in enumerate(NEXT[n + 1] if n + 1 < NS else ()):
                if (h, sub) == (after, subs(s, h)[0]):
                    pz(n + 1, s, 1, subs(s, 1)[i])
                    if s > 0 and i:
                        send(("PC", n + 1, 0, 0), "c")
        elif kind == "AR1":
            k = key[1]
            y = "y" + "+-"[k]
            send(("AR2", k), y)
            for zz in (0, 1):
                send(("AY", 1 - 2 * k, zz), y)
            for n in EARLY:
                send(("PY", n, 1 - 2 * k, 1), y)
        elif kind == "PY" and key[3] == 1:
            send(("PY", key[1], key[2], 2), "y" + sgn(key[2]), 0.5)
        elif kind in ("AY", "AR2"):
            held.append(((-key[1]) % NY, key[2]) if kind == "AY" else (2, key[1]))
            forward_x()
        elif kind == "XS":
            _, d, zz, s, h = key
            if h == 1 and (zz == 0) == (s > 0):
                send(("XS", d, zz, s, 2), "x" + sgn(s))
            if h == 1:
                under_way[(d, zz)] -= 1
                if not under_way[(d, zz)]:
                    del under_way[(d, zz)]
                    forward_x()

    waited, times = set(), []

    def receive(key):
        program.append(("recv",) + key)
        clock[0] += T_ISSUE
        waited.add(key)
        times.append((clock[0],) + key)

    def passes_on(key):
        if key[0] == "XS":
            return key[4] == 1
        if key[0] == "PY":
            return key[3] == 1
        return key[0] in ("PZ", "AR1", "AR2", "AY")

    for s in (1, -1):
        start_slice(0, s)
        send(("AR1", 0 if s > 0 else 1), "y" + sgn(s))
        send(("XS", 0, 0, s, 1), "x" + sgn(s))
    send(("PC", 0, 0, 0), "c")
    for s in (1, -1):
        send(("XS", 0, 1, s, 1), "x" + sgn(s))
    program.append(("local",))

    jobs = {}
    arrive = {n: {} for n in range(NS)}
    for n in range(NS):
        arrive[n][0] = {("PC", n, 0, 0)}
        for s in (1, -1):
            for h in range(1, FAR + 1):
                for sub in subs(s, h):
                    rel = (-s * h) % NZ
                    arrive[n].setdefault(rel, set()).update({("PZ", n, s, h, sub), ("PC", n, rel, sub + 1 if h == FAR else 0)})
    rows = {}
    for d in range(NY):
        need = {("XS", d, zz, s, 1) for zz in (0, 1) for s in (1, -1)} | {("XS", d, 0, 1, 2), ("XS", d, 1, -1, 2)}
        side = 1 if d == 3 else -1
        rows[d] = need | {0: set(), 2: {("AR2", 0), ("AR2", 1)}}.get(d, {("AY", side, 0), ("AY", side, 1)})
    ready_rows = {("prepA", d) for d in range(NY) if d != LATE_D}
    for d in range(NY):
        if d != LATE_D:
            jobs[("prepA", d)] = (-1.0, rows[d], T_PREP * 8)
    blocks = {("block", 0, zz): {("AY", -1, zz)} for zz in (0, 1)}
    blocks |= {("block", (-s) % NX, zz): {("XS", LATE_D, zz, s, 1)} for zz in (0, 1) for s in (1, -1)}
    blocks |= {("block", 2, 0): {("XS", LATE_D, 0, 1, 2)}, ("block", 2, 1): {("XS", LATE_D, 1, -1, 2)}}
    for job, need in blocks.items():
        jobs[job] = (-1.5, need | {("prepB", n) for n in range(NS) if n not in STEPPED}, T_BLOCK)
    early = {("PY", n, s, h) for n in EARLY for s in (1, -1) for h in (1, 2)}
    for n in range(NS):
        whole = n == NS - 1
        if n in STEPPED:
            steps = {("step", n, rel) for rel in range(NZ)}
            for rel in range(NZ):
                jobs[("step", n, rel)] = (n - 0.5, arrive[n][rel] | ready_rows | (set(blocks) if whole else set()), T_STEP if whole else T_BLOCK)
        else:
            jobs[("prepB", n)] = (-2.0, set().union(*arrive[n].values()), T_PREP * 16)
        done = {}
        for d in range(NY):
            if n not in STEPPED and d == LATE_D:
                done[d] = set(blocks)
            elif n in STEPPED and (whole or d != LATE_D):
                done[d] = steps
            else:
                done[d] = {("task", d, n)}
                need = set(blocks) | steps if n in STEPPED else {("prepA", d), ("prepB", n)}
                jobs[("task", d, n)] = (n + 0.1 * POS[d] - (1 if d == 2 else 0), need, T_TASK)
        everything = set().union(*done.values())
        first = ("vpart", n)
        if n in EARLY:
            jobs[first] = (-3.5, everything | early, 0.15)
        jobs[("y2", n)] = (-3.0, done[2], 0.0)
        for s in (1, -1):
            jobs[("y0", n, s)] = (-2.9, done[s % NY], 0.0)
            jobs[("y1", n, s)] = (-3.0, ({first} if n in EARLY else done[s % NY]) | {("Y2", n, s)}, T_SMALL)
        jobs[("fin", n)] = (-3.0, ({first} if n in EARLY else done[0]) | {("Y1", n, s, i) for s in (1, -1) for i in (0, 1)}, T_SMALL)
    jobs[("vz",)] = (-4.0, {("vpart", n) for n in EARLY} | {("fin", n) for n in range(NS) if n not in EARLY}, 0.0)
    jobs[("vg",)] = (-4.0, {("VZ",)}, 0.05)
    jobs[("vend",)] = (-4.0, {("VG",)}, 0.05)
    while jobs or arrivals:
        if arrivals and arrivals[0][0] <= clock[0]:
            key = heapq.heappop(arrivals)[2]
            got.add(key)
            if passes_on(key):
                receive(key)
                on(key)
            continue
        ready = [(p, j) for j, (p, need, _) in jobs.items() if need <= got]
        if ready:
            job = min(ready, key=lambda r: (r[0], str(r[1])))[1]
            for key in sorted(jobs[job][1], key=str):
                if key[0].isupper() and key not in waited:
                    receive(key)
            program.append(job)
            times.append((clock[0],) + job)
            clock[0] += jobs.pop(job)[2]
            got.add(job)
            if job[0] == "y2":
                for s in (1, -1):
                    send(("Y2", job[1], s), "y" + sgn(s), 0.5)
            elif job[0] == "y1":
                send(("Y1", job[1], job[2], 1), "y" + sgn(job[2]), 0.5)
            elif job[0] == "y0":
                send(("Y1", job[1], job[2], 0), "y" + sgn(job[2]), 0.5)
            elif job[0] in ("vz", "vg"):
                send((job[0].upper(),), job[0])
            continue
        late = sorted((t, k) for k, t in done_at.items() if t + 3.0 < clock[0])
        if late and arrivals and arrivals[0][0] > clock[0] + 0.1:
            program.append(("sent",) + late[0][1])
            del done_at[late[0][1]]
            clock[0] += 0.03
            continue
        clock[0] = max(clock[0], arrivals[0][0])

    final, slots, pool, flying = [], {}, list(range(SEND_POOL)), []
    for act in program:
        key = act[1:]
        if act[0] == "send" and key[0] not in ("VZ", "VG"):
            if not pool:
                old = min(flying, key=lambda k: (ends[k], str(k)))
                final.append(("sent",) + old)
                flying.remove(old)
                pool.append(slots[old])
            slots[key] = pool.pop(0)
            flying.append(key)
        if act[0] == "sent":
            if key not in flying:
                continue
            flying.remove(key)
            pool.append(slots[key])
        final.append(act)
    for key in flying + [("VZ",), ("VG",)]:
        final.append(("sent",) + key)
    return final, slots, clock[0], free, times


def kernel(program, slots, sem_of, pattern_hbm, sigma, panel, cross, var, pattern, pbuf, sbuf, relay, a_hi, a_lo, b_hi, b_lo, part, r1, r2,
           pv, vz, vg, send_sem, recv_sem, local_sem):
    row, x = lax.axis_index("row"), lax.axis_index("col")
    z, y, c = row // (2 * NY), (row // 2) % NY, row % 2
    flip_y = 1 - 2 * c

    def at(dx=0, dy=0, dz=0, flip=False):
        core = 1 - c if flip else c
        return ((((z + dz + NZ) % NZ) * NY + (y + flip_y * dy + NY) % NY) * 2 + core, (x + dx + NX) % NX)

    halves = [pl.ds(0, B // 2), pl.ds(B // 2, B // 2)]

    def lanes(start):
        return pl.ds(pl.multiple_of(start, W), W)

    def ends(key, sender):
        kind = key[0]
        if kind == "PZ":
            _, n, s, h, sub = key
            zs = (z - s * (h - 1 if sender else h) + NZ) % NZ
            dst = pbuf.at[n, 2 * zs + c, halves[sub]]
            src = panel.at[halves[sub], pl.ds(n * W, W)] if h == 1 else dst
            return src, dst, at(dz=s)
        if kind == "PC":
            _, n, rel, part_no = key
            zs = (z + rel) % NZ
            dst = pbuf.at[n, 2 * zs + (c if sender else 1 - c)]
            if part_no:
                dst = pbuf.at[n, 2 * zs + (c if sender else 1 - c), halves[part_no - 1]]
            src = panel.at[:, pl.ds(n * W, W)] if rel == 0 else dst
            return src, dst, at(flip=True)
        if kind == "AY":
            _, s, zz = key
            src = sigma.at[:, lanes(zz * NY * W + ((y + flip_y * s + NY) % NY) * W)]
            return src, sbuf.at[(-s) % NY, 2 * x + zz], at(dy=s)
        if kind == "AR1":
            k = key[1]
            src = sigma.at[:, lanes(k * NY * W + ((y + 2) % NY) * W)]
            return src, relay.at[k], at(dy=1 - 2 * k)
        if kind == "AR2":
            k = key[1]
            return relay.at[k], sbuf.at[2, 2 * x + k], at(dy=1 - 2 * k)
        if kind == "XS":
            _, d, zz, s, h = key
            xs = (x - s * (h - 1 if sender else h) + NX) % NX
            dst = sbuf.at[d, 2 * xs + zz]
            src = sigma.at[:, lanes(zz * NY * W + y * W)] if d == 0 and h == 1 else dst
            return src, dst, at(dx=s)
        if kind == "PY":
            _, n, s, h = key
            e = EARLY.index(n)
            if h == 1:
                return panel.at[:, pl.ds(n * W, W)], pv.at[e, (-s) % NY], at(dy=s)
            half = halves[(1 - s) // 2]
            return pv.at[e, (-s) % NY, half], pv.at[e, 2, half], at(dy=s)
        if kind == "Y2":
            _, n, s = key
            i = 0 if s > 0 else 1
            return part.at[n, POS[2], pl.ds(i * (B // 2), B // 2)], r1.at[i, n], at(dy=s)
        _, n, s, i = key
        half = halves[(1 - s) // 2 if i else (1 + s) // 2]
        return part.at[n, POS[s % NY], half], r2.at[0 if s > 0 else 1, n, half], at(dy=s)

    def copy(key, sender):
        src, dst, target = ends(key, sender)
        return pltpu.make_async_remote_copy(
            src_ref=src if sender else dst, dst_ref=dst, send_sem=send_sem.at[slots[key]], recv_sem=recv_sem.at[sem_of[key]],
            device_id=target, device_id_type=MESH)

    def column_sums(kind, ref=None, peer=None):
        buf, mine = (vz, z) if kind == "VZ" else (vg, me8)
        ref = buf.at[pl.ds(0, 7)] if peer is None else buf.at[mine]
        i = 0 if kind == "VZ" else 1
        return pltpu.make_async_remote_copy(
            src_ref=ref, dst_ref=ref, send_sem=send_sem.at[SEND_POOL + i], recv_sem=recv_sem.at[sem_of[(kind,)]],
            device_id=at(dz=1) if peer is None else peer, device_id_type=MESH)

    me8 = row % (2 * NY)
    barrier = pltpu.get_barrier_semaphore()
    peers = [at(dx=1), at(dx=-1), at(dy=1), at(dy=-1), at(dz=1), at(dz=-1), at(flip=True)]
    for peer in peers:
        pl.semaphore_signal(barrier, inc=1, device_id=peer, device_id_type=MESH)
    locals_ = [pltpu.make_async_copy(panel.at[:, pl.ds(n * W, W)], pbuf.at[n, 2 * z + c], local_sem.at[n]) for n in range(NS)]
    locals_ += [pltpu.make_async_copy(sigma.at[:, lanes(zz * NY * W + y * W)], sbuf.at[0, 2 * x + zz], local_sem.at[NS + zz]) for zz in (0, 1)]
    locals_ += [pltpu.make_async_copy(pattern_hbm, pattern, local_sem.at[NS + 2])]
    pl.semaphore_wait(barrier, len(peers))

    def split_a(d, zk):
        rb = (z * NY + (y + flip_y * d + NY) % NY) * 2 + c
        cb = (zk * NY + y) * 2
        for j in (0, 1):
            m = pattern[rb, cb + j].astype(F32)
            v = sbuf[d, zk, :, pl.ds(j * B, B)] * m
            hi = v.astype(BF16)
            a_hi[zk, pl.ds(POS[d] * B, B), pl.ds(j * B, B)] = hi
            a_lo[zk, pl.ds(POS[d] * B, B), pl.ds(j * B, B)] = (v - hi.astype(F32)).astype(BF16)

    def prep_a(d):
        def one(zk, carry):
            split_a(d, zk)
            return carry

        lax.fori_loop(0, NZ, one, 0)

    def split_b(n, k):
        for j in (0, 1):
            p = pbuf[n, 2 * k + j]
            hi = p.astype(BF16)
            b_hi[n, k, pl.ds(j * B, B)] = hi
            b_lo[n, k, pl.ds(j * B, B)] = (p - hi.astype(F32)).astype(BF16)

    def prep_b(n):
        def one(k, carry):
            split_b(n, k)
            return carry

        lax.fori_loop(0, NZ, one, 0)

    dot = functools.partial(jnp.dot, preferred_element_type=F32)

    def product(n, k, lo, hi):
        ah, al = a_hi[k, pl.ds(lo * B, (hi - lo) * B)], a_lo[k, pl.ds(lo * B, (hi - lo) * B)]
        return dot(ah, b_hi[n, k]) + (dot(ah, b_lo[n, k]) + dot(al, b_hi[n, k]))

    begun = set()

    def add_product(n, k, lo, hi):
        res = product(n, k, lo, hi).reshape(hi - lo, B, W)
        part[n, pl.ds(lo, hi - lo)] = part[n, pl.ds(lo, hi - lo)] + res if (n, lo) in begun else res
        begun.add((n, lo))

    def task(d, n):
        acc = jnp.zeros((B, W), F32)
        for k in range(NZ):
            acc = acc + product(n, k, POS[d], POS[d] + 1)
        part[n, POS[d]] = acc

    def step(n, rel):
        k = (z + rel) % NZ
        split_b(n, k)
        add_product(n, k, 0, NY if n == NS - 1 else NY - 1)

    def block(xr, zz):
        k = 2 * ((x + xr) % NX) + zz
        split_a(LATE_D, k)
        for n in range(NS):
            if n not in STEPPED:
                add_product(n, k, POS[LATE_D], POS[LATE_D] + 1)

    def put_var(n, prod):
        for j in (0, 1):
            vz[z, pl.ds(2 * n + j, 1)] = prod[:, j * B:(j + 1) * B]

    for act in program:
        kind = act[0]
        if kind == "send":
            if act[1] == "VZ":
                for r in range(1, NZ):
                    column_sums("VZ", peer=at(dz=r)).start()
            elif act[1] == "VG":
                for r in range(1, 2 * NY):
                    column_sums("VG", peer=(z * 2 * NY + (me8 + r) % (2 * NY), x)).start()
            else:
                copy(act[1:], True).start()
        elif kind == "recv":
            if act[1] in ("VZ", "VG"):
                column_sums(act[1]).wait_recv()
            else:
                copy(act[1:], False).wait_recv()
        elif kind == "sent":
            if act[1] in ("VZ", "VG"):
                column_sums(act[1]).wait_send()
            else:
                copy(act[1:], True).wait_send()
        elif kind == "local":
            for cp in locals_:
                cp.start()
            for cp in locals_:
                cp.wait()
        elif kind == "prepA":
            prep_a(act[1])
        elif kind == "prepB":
            prep_b(act[1])
        elif kind == "task":
            task(act[1], act[2])
        elif kind == "step":
            step(act[1], act[2])
        elif kind == "block":
            block(act[1], act[2])
        elif kind == "y1":
            _, n, s = act
            i = 0 if s > 0 else 1
            half = pl.ds(i * (B // 2), B // 2)
            part[n, POS[s % NY], half] = part[n, POS[s % NY], half] + r1[i, n]
        elif kind == "fin":
            n = act[1]
            out = part[n, 0] + (r2[0, n] + r2[1, n])
            cross[:, pl.ds(n * W, W)] = out
            if n not in EARLY:
                put_var(n, jnp.sum(out * pbuf[n, 2 * z + c], axis=0, keepdims=True))
        elif kind == "vpart":
            n = act[1]
            prod = part[n, 0] * pbuf[n, 2 * z + c]
            for d in range(1, NY):
                prod = prod + part[n, POS[d]] * pv[EARLY.index(n), d]
            put_var(n, jnp.sum(prod, axis=0, keepdims=True))
        elif kind == "vg":
            total = vz[0]
            for i in range(1, NZ):
                total = total + vz[i]
            vg[me8] = total
        elif kind == "vend":
            total = vg[0]
            for i in range(1, 2 * NY):
                total = total + vg[i]
            var[...] = total


def body(sigma_anc, panel_hat, pattern, diag_inverse):
    program, slots = plan()[:2]
    keys = sorted({act[1:] for act in program if act[0] == "send"}, key=str)
    sem_of = {key: i for i, key in enumerate(keys)}
    dma = pltpu.SemaphoreType.DMA
    vmem = pl.BlockSpec(memory_space=pltpu.VMEM)
    cross, var = pl.pallas_call(
        functools.partial(kernel, program, slots, sem_of),
        out_shape=(pltpu.VMEM((B, NS * W), F32), pltpu.VMEM((8, B), F32)),
        in_specs=[pl.BlockSpec(memory_space=pltpu.HBM)] * 3,
        out_specs=(vmem, vmem),
        scratch_shapes=[
            pltpu.SMEM((NY * NZ * 2, NY * NZ * 2), jnp.int32),
            pltpu.VMEM((NS, 2 * NZ, B, W), F32),
            pltpu.VMEM((NY, NZ, B, W), F32),
            pltpu.VMEM((2, B, W), F32),
            pltpu.VMEM((NZ, NY * B, W), BF16),
            pltpu.VMEM((NZ, NY * B, W), BF16),
            pltpu.VMEM((NS, NZ, W, W), BF16),
            pltpu.VMEM((NS, NZ, W, W), BF16),
            pltpu.VMEM((NS, NY, B, W), F32),
            pltpu.VMEM((2, NS, B // 2, W), F32),
            pltpu.VMEM((2, NS, B, W), F32),
            pltpu.VMEM((len(EARLY), NY, B, W), F32),
            pltpu.VMEM((NZ, 8, B), F32),
            pltpu.VMEM((2 * NY, 8, B), F32),
            dma((SEND_POOL + 2,)),
            dma((len(keys),)),
            dma((NS + 3,)),
        ],
        compiler_params=pltpu.CompilerParams(collective_id=0, has_side_effects=True, vmem_limit_bytes=56 * 1024 * 1024),
        name="selected_inverse",
    )(pattern, sigma_anc, panel_hat)
    return -cross, diag_inverse + var.reshape(-1)


def solution(mesh):
    in_specs = (P("row", "col"), P("row", "col"), P(), P("col"))
    out_specs = (P("row", "col"), P("col"))
    return jax.shard_map(body, mesh=mesh, in_specs=in_specs, out_specs=out_specs, check_vma=False)
```

```python
import functools
import heapq

import jax
import jax.numpy as jnp
from jax import lax
from jax.experimental import pallas as pl
from jax.experimental.pallas import tpu as pltpu
from jax.sharding import PartitionSpec as P

MESH = pl.DeviceIdType.MESH
NX, NY, NZ = 4, 4, 8
B = 128
W = 256
NS = 4
F32, BF16 = jnp.float32, jnp.bfloat16

EARLY = (0, 1, 2, 3)
STEPPED = (2, 3)
LATE_D = 1
POS = (0, 3, 1, 2)
FAR = NZ // 2
SEND_POOL = 40
FIN = 2.6
Y_SHARED = 25.0
X_WINDOW = 2
NEXT = (None, (1, 2), (1, 2), (2, 2))

LINK, LAT, CORE, CORE_LAT = 2.84, 2.1, 0.3, 1.0
T_ISSUE, T_PREP, T_TASK, T_SMALL, T_STEP, T_PART, T_BLOCK = 0.02, 0.035, 0.97, 0.05, 0.48, 0.36, 0.24
VZ_LAT, VG_LAT = 4.2, 3.0
D_ORDER = (0, 2, 3, 1)


def subs(s, h):
    first = 0 if s > 0 else 1
    return (first,) if h == FAR else (first, 1 - first)


def sgn(s):
    return "+" if s > 0 else "-"


def plan():
    program, arrivals, free, done_at = [], [], {}, {}
    clock = [0.0]
    got, seq, ends = set(), [0], {}

    def send(key, link, units=1.0):
        program.append(("send",) + key)
        clock[0] += T_ISSUE
        cost, lat = {"c": (CORE, CORE_LAT), "vz": (0.0, VZ_LAT), "vg": (0.0, VG_LAT)}.get(link, (LINK, LAT))
        start = max(clock[0], free.get(link, 0.0))
        if link == "vg":
            start = max([start] + [free.get(other, 0.0) for other in ("y+", "y-")])
        took = cost * units
        if link[0] == "y" and clock[0] > Y_SHARED:
            both = min(max(free.get("y+" if link == "y-" else "y-", 0.0) - start, 0.0), took)
            took = (took + both) / 2
        free[link] = start + took
        done_at[key] = ends[key] = free[link]
        seq[0] += 1
        heapq.heappush(arrivals, (free[link] + lat, seq[0], key))

    def pz(n, s, h, sub):
        send(("PZ", n, s, h, sub), "z" + sgn(s), 0.5)

    def start_slice(n, s):
        for sub in subs(s, 1):
            pz(n, s, 1, sub)

    order = {d: i for i, d in enumerate(D_ORDER)}
    held, under_way = [], {(0, 0): 2, (0, 1): 2}

    def forward_x():
        while held and len(under_way) < X_WINDOW:
            d, zz = min(held, key=lambda e: (order[e[0]], e[1]))
            if any(("own", e, f) not in got for e in D_ORDER[1:order[d]] for f in (0, 1)):
                return
            held.remove((d, zz))
            got.add(("own", d, zz))
            under_way[(d, zz)] = 2
            for s in (1, -1):
                send(("XS", d, zz, s, 1), "x" + sgn(s))

    def on(key):
        kind = key[0]
        if kind == "PZ":
            _, n, s, h, sub = key
            if h < FAR and sub in subs(s, h + 1):
                pz(n, s, h + 1, sub)
            if h == FAR:
                send(("PC", n, FAR, sub + 1), "c", 0.5)
            elif sub == subs(s, h)[1]:
                send(("PC", n, (-s * h) % NZ, 0), "c")
            for i, after in enumerate(NEXT[n + 1] if n + 1 < NS else ()):
                if (h, sub) == (after, subs(s, h)[0]):
                    pz(n + 1, s, 1, subs(s, 1)[i])
                    if s > 0 and i:
                        send(("PC", n + 1, 0, 0), "c")
        elif kind == "AR1":
            _, k, sub = key
            y = "y" + "+-"[k]
            send(("AR2", k, sub), y, 0.5)
            if not sub:
                return
            for zz in (0, 1):
                send(("AY", 1 - 2 * k, zz), y)
            for n in EARLY[:2]:
                send(("PY", n, 1 - 2 * k, 1), y)
        elif kind == "PY" and key[3] == 1:
            send(("PY", key[1], key[2], 2), "y" + sgn(key[2]), 0.5)
            if EARLY.index(key[1]) + 2 < len(EARLY):
                send(("PY", EARLY[EARLY.index(key[1]) + 2], key[2], 1), "y" + sgn(key[2]))
        elif kind in ("AY", "AR2"):
            if kind == "AR2" and not {("AR2", key[1], sub) for sub in (0, 1)} <= waited:
                return
            held.append(((-key[1]) % NY, key[2]) if kind == "AY" else (2, key[1]))
            forward_x()
        elif kind == "XS":
            _, d, zz, s, h = key
            if h == 1 and (zz == 0) == (s > 0):
                send(("XS", d, zz, s, 2), "x" + sgn(s))
            if h == 1:
                under_way[(d, zz)] -= 1
                if not under_way[(d, zz)]:
                    del under_way[(d, zz)]
                    forward_x()

    waited, times = set(), []

    def receive(key):
        program.append(("recv",) + key)
        clock[0] += T_ISSUE
        waited.add(key)
        times.append((clock[0],) + key)

    def passes_on(key):
        if key[0] == "XS":
            return key[4] == 1
        if key[0] == "PY":
            return key[3] == 1
        return key[0] in ("PZ", "AR1", "AR2", "AY")

    for s in (1, -1):
        start_slice(0, s)
        for sub in (0, 1):
            send(("AR1", 0 if s > 0 else 1, sub), "y" + sgn(s), 0.5)
        send(("XS", 0, 0, s, 1), "x" + sgn(s))
    send(("PC", 0, 0, 0), "c")
    for s in (1, -1):
        send(("XS", 0, 1, s, 1), "x" + sgn(s))
    program.append(("local",))

    jobs = {}
    arrive = {n: {} for n in range(NS)}
    for n in range(NS):
        arrive[n][0] = {("PC", n, 0, 0)}
        for s in (1, -1):
            for h in range(1, FAR + 1):
                for sub in subs(s, h):
                    rel = (-s * h) % NZ
                    arrive[n].setdefault(rel, set()).update({("PZ", n, s, h, sub), ("PC", n, rel, sub + 1 if h == FAR else 0)})
    rows = {}
    for d in range(NY):
        need = {("XS", d, zz, s, 1) for zz in (0, 1) for s in (1, -1)} | {("XS", d, 0, 1, 2), ("XS", d, 1, -1, 2)}
        side = 1 if d == 3 else -1
        rows[d] = need | {0: set(), 2: {("AR2", k, sub) for k in (0, 1) for sub in (0, 1)}}.get(d, {("AY", side, 0), ("AY", side, 1)})
    ready_rows = {("prepA", d) for d in range(NY) if d != LATE_D}
    for d in range(NY):
        if d != LATE_D:
            jobs[("prepA", d)] = (-1.0, rows[d], T_PREP * 8)
    blocks = {("block", 0, zz): {("AY", -1, zz)} for zz in (0, 1)}
    blocks |= {("block", (-s) % NX, zz): {("XS", LATE_D, zz, s, 1)} for zz in (0, 1) for s in (1, -1)}
    blocks |= {("block", 2, 0): {("XS", LATE_D, 0, 1, 2)}, ("block", 2, 1): {("XS", LATE_D, 1, -1, 2)}}
    for job, need in blocks.items():
        jobs[job] = (-1.5, need | {("prepB", n) for n in range(NS) if n not in STEPPED}, T_BLOCK)
    for n in range(NS):
        whole = n == NS - 1
        if n in STEPPED:
            steps = {("step", n, rel) for rel in range(NZ)}
            for rel in range(NZ):
                jobs[("step", n, rel)] = (n - 0.5, arrive[n][rel] | ready_rows | (set(blocks) if whole else set()), T_STEP if whole else T_PART)
        else:
            jobs[("prepB", n)] = (-2.0, set().union(*arrive[n].values()), T_PREP * 16)
        done = {}
        for d in range(NY):
            if n not in STEPPED and d == LATE_D:
                done[d] = set(blocks)
            elif n in STEPPED and (whole or d != LATE_D):
                done[d] = steps
            else:
                done[d] = {("task", d, n)}
                need = set(blocks) | steps if n in STEPPED else {("prepA", d), ("prepB", n)}
                jobs[("task", d, n)] = (n + 0.1 * POS[d] - (1 if d == 2 else 0), need, T_TASK)
        everything = set().union(*done.values())
        first = ("vpart", n)
        if n in EARLY:
            jobs[first] = (-3.5, everything | {("PY", n, s, h) for s in (1, -1) for h in (1, 2)}, 0.1)
        jobs[("y2", n)] = (-3.0, done[2], 0.0)
        for s in (1, -1):
            jobs[("y0", n, s)] = (-2.9, done[s % NY], 0.0)
            jobs[("y1", n, s)] = (-3.0, done[s % NY] | {("Y2", n, s)}, T_SMALL)
        jobs[("fin", n)] = (FIN, ({first} if n in EARLY else done[0]) | {("Y1", n, s, i) for s in (1, -1) for i in (0, 1)}, T_SMALL)
    jobs[("v1",)] = (-4.0, {("vpart", n) for n in EARLY} | {("fin", n) for n in range(NS) if n not in EARLY}, 0.0)
    jobs[("v2",)] = (-4.0, {("VG",)}, 0.05)
    jobs[("vend",)] = (-4.0, {("VZ",)}, 0.05)
    while jobs or arrivals:
        if arrivals and arrivals[0][0] <= clock[0]:
            key = heapq.heappop(arrivals)[2]
            got.add(key)
            if passes_on(key):
                receive(key)
                on(key)
            continue
        ready = [(p, j) for j, (p, need, _) in jobs.items() if need <= got]
        if ready:
            job = min(ready, key=lambda r: (r[0], str(r[1])))[1]
            for key in sorted(jobs[job][1], key=str):
                if key[0].isupper() and key not in waited:
                    receive(key)
            program.append(job)
            times.append((clock[0],) + job)
            clock[0] += jobs.pop(job)[2]
            got.add(job)
            if job[0] == "y2":
                for s in (1, -1):
                    send(("Y2", job[1], s), "y" + sgn(s), 0.5)
            elif job[0] == "y1":
                send(("Y1", job[1], job[2], 1), "y" + sgn(job[2]), 0.5)
            elif job[0] == "y0":
                send(("Y1", job[1], job[2], 0), "y" + sgn(job[2]), 0.5)
            elif job[0] == "v1":
                send(("VG",), "vg")
            elif job[0] == "v2":
                send(("VZ",), "vz")
            continue
        late = sorted((t, k) for k, t in done_at.items() if t + 3.0 < clock[0])
        if late and arrivals and arrivals[0][0] > clock[0] + 0.1:
            program.append(("sent",) + late[0][1])
            del done_at[late[0][1]]
            clock[0] += 0.03
            continue
        clock[0] = max(clock[0], arrivals[0][0])

    final, slots, pool, flying = [], {}, list(range(SEND_POOL)), []
    for act in program:
        key = act[1:]
        if act[0] == "send" and key[0] not in ("VZ", "VG"):
            if not pool:
                old = min(flying, key=lambda k: (ends[k], str(k)))
                final.append(("sent",) + old)
                flying.remove(old)
                pool.append(slots[old])
            slots[key] = pool.pop(0)
            flying.append(key)
        if act[0] == "sent":
            if key not in flying:
                continue
            flying.remove(key)
            pool.append(slots[key])
        final.append(act)
    for key in flying + [("VZ",), ("VG",)]:
        final.append(("sent",) + key)
    return final, slots, clock[0], free, times


def receive_slots(program):
    at = {act: i for i, act in enumerate(program)}
    keys = [act[1:] for act in program if act[0] == "send"]

    def channel(key):
        if key[0] == "PC":
            return "c", 0
        if key[0] in ("AR1", "AR2"):
            return "y", 1 - 2 * key[1]
        return {"P": "z", "X": "x", "A": "y", "Y": "y"}["Y" if key[0] == "PY" else key[0][0]], key[{"PZ": 2, "XS": 3, "AY": 1, "PY": 2, "Y2": 2, "Y1": 2}[key[0]]]

    slots, users = {}, []
    for key in keys:
        if key[0] in ("VZ", "VG"):
            users.append(None)
            slots[key] = len(users) - 1
            continue
        axis, s = channel(key)
        back = [m for m in keys if m[0] not in ("VZ", "VG") and channel(m) == (axis, -s)]
        free = None
        for i, last in enumerate(users):
            if last is None or channel(last) != (axis, s):
                continue
            if any(at[("send",) + m] > at[("recv",) + last] and at[("recv",) + m] < at[("send",) + key] for m in back):
                free = i
                break
        if free is None:
            users.append(key)
            free = len(users) - 1
        users[free] = key
        slots[key] = free
    return slots


def kernel(program, slots, sem_of, pattern_hbm, sigma, panel, diag_hbm, cross, var, diag, pattern, pbuf, sbuf, relay, a_hi, a_lo, b_hi, b_lo, part, r1, r2,
           pv, vz, vg, send_sem, recv_sem, local_sem):
    row, x = lax.axis_index("row"), lax.axis_index("col")
    z, y, c = row // (2 * NY), (row // 2) % NY, row % 2
    flip_y = 1 - 2 * c

    def at(dx=0, dy=0, dz=0, flip=False):
        core = 1 - c if flip else c
        return ((((z + dz + NZ) % NZ) * NY + (y + flip_y * dy + NY) % NY) * 2 + core, (x + dx + NX) % NX)

    halves = [pl.ds(0, B // 2), pl.ds(B // 2, B // 2)]

    def lanes(start):
        return pl.ds(pl.multiple_of(start, W), W)

    def ends(key, sender):
        kind = key[0]
        if kind == "PZ":
            _, n, s, h, sub = key
            zs = (z - s * (h - 1 if sender else h) + NZ) % NZ
            dst = pbuf.at[n, 2 * zs + c, halves[sub]]
            src = panel.at[halves[sub], pl.ds(n * W, W)] if h == 1 else dst
            return src, dst, at(dz=s)
        if kind == "PC":
            _, n, rel, part_no = key
            zs = (z + rel) % NZ
            dst = pbuf.at[n, 2 * zs + (c if sender else 1 - c)]
            if part_no:
                dst = pbuf.at[n, 2 * zs + (c if sender else 1 - c), halves[part_no - 1]]
            src = panel.at[:, pl.ds(n * W, W)] if rel == 0 else dst
            return src, dst, at(flip=True)
        if kind == "AY":
            _, s, zz = key
            src = sigma.at[:, lanes(zz * NY * W + ((y + flip_y * s + NY) % NY) * W)]
            return src, sbuf.at[(-s) % NY, 2 * x + zz], at(dy=s)
        if kind == "AR1":
            _, k, sub = key
            src = sigma.at[halves[sub], lanes(k * NY * W + ((y + 2) % NY) * W)]
            return src, relay.at[k, halves[sub]], at(dy=1 - 2 * k)
        if kind == "AR2":
            _, k, sub = key
            return relay.at[k, halves[sub]], sbuf.at[2, 2 * x + k, halves[sub]], at(dy=1 - 2 * k)
        if kind == "XS":
            _, d, zz, s, h = key
            xs = (x - s * (h - 1 if sender else h) + NX) % NX
            dst = sbuf.at[d, 2 * xs + zz]
            src = sigma.at[:, lanes(zz * NY * W + y * W)] if d == 0 and h == 1 else dst
            return src, dst, at(dx=s)
        if kind == "PY":
            _, n, s, h = key
            e = EARLY.index(n)
            if h == 1:
                return panel.at[:, pl.ds(n * W, W)], pv.at[e, (-s) % NY], at(dy=s)
            half = halves[(1 - s) // 2]
            return pv.at[e, (-s) % NY, half], pv.at[e, 2, half], at(dy=s)
        if kind == "Y2":
            _, n, s = key
            i = 0 if s > 0 else 1
            return part.at[n, POS[2], pl.ds(i * (B // 2), B // 2)], r1.at[i, n], at(dy=s)
        _, n, s, i = key
        half = halves[(1 - s) // 2 if i else (1 + s) // 2]
        side = 0 if s > 0 else 1
        return r1.at[side, n] if i else part.at[n, POS[s % NY], half], r2.at[0 if s > 0 else 1, n, half], at(dy=s)

    def copy(key, sender):
        src, dst, target = ends(key, sender)
        return pltpu.make_async_remote_copy(
            src_ref=src if sender else dst, dst_ref=dst, send_sem=send_sem.at[slots[key]], recv_sem=recv_sem.at[sem_of[key]],
            device_id=target, device_id_type=MESH)

    def column_sums(kind, ref=None, peer=None):
        buf, mine = (vz, z) if kind == "VZ" else (vg, me8)
        ref = buf.at[pl.ds(0, 7)] if peer is None else buf.at[mine]
        i = 0 if kind == "VZ" else 1
        return pltpu.make_async_remote_copy(
            src_ref=ref, dst_ref=ref, send_sem=send_sem.at[SEND_POOL + i], recv_sem=recv_sem.at[sem_of[(kind,)]],
            device_id=at(dz=1) if peer is None else peer, device_id_type=MESH)

    me8 = row % (2 * NY)
    barrier = pltpu.get_barrier_semaphore()
    peers = [at(dx=1), at(dx=-1), at(dy=1), at(dy=-1), at(dz=1), at(dz=-1), at(flip=True)]
    for peer in peers:
        pl.semaphore_signal(barrier, inc=1, device_id=peer, device_id_type=MESH)
    locals_ = [pltpu.make_async_copy(panel.at[:, pl.ds(n * W, W)], pbuf.at[n, 2 * z + c], local_sem.at[n]) for n in range(NS)]
    locals_ += [pltpu.make_async_copy(sigma.at[:, lanes(zz * NY * W + y * W)], sbuf.at[0, 2 * x + zz], local_sem.at[NS + zz]) for zz in (0, 1)]
    locals_ += [pltpu.make_async_copy(pattern_hbm, pattern, local_sem.at[NS + 2])]
    locals_ += [pltpu.make_async_copy(diag_hbm, diag, local_sem.at[NS + 3])]
    pl.semaphore_wait(barrier, len(peers))

    def split_a(d, zk):
        rb = (z * NY + (y + flip_y * d + NY) % NY) * 2 + c
        cb = (zk * NY + y) * 2
        for j in (0, 1):
            m = pattern[rb, cb + j].astype(F32)
            v = sbuf[d, zk, :, pl.ds(j * B, B)] * m
            hi = v.astype(BF16)
            a_hi[zk, pl.ds(POS[d] * B, B), pl.ds(j * B, B)] = hi
            a_lo[zk, pl.ds(POS[d] * B, B), pl.ds(j * B, B)] = (v - hi.astype(F32)).astype(BF16)

    def prep_a(d):
        def one(zk, carry):
            split_a(d, zk)
            return carry

        lax.fori_loop(0, NZ, one, 0)

    def split_b(n, k):
        for j in (0, 1):
            p = pbuf[n, 2 * k + j]
            hi = p.astype(BF16)
            b_hi[n, k, pl.ds(j * B, B)] = hi
            b_lo[n, k, pl.ds(j * B, B)] = (p - hi.astype(F32)).astype(BF16)

    def prep_b(n):
        def one(k, carry):
            split_b(n, k)
            return carry

        lax.fori_loop(0, NZ, one, 0)

    dot = functools.partial(jnp.dot, preferred_element_type=F32)

    def product(n, k, lo, hi):
        ah, al = a_hi[k, pl.ds(lo * B, (hi - lo) * B)], a_lo[k, pl.ds(lo * B, (hi - lo) * B)]
        return dot(ah, b_hi[n, k]) + (dot(ah, b_lo[n, k]) + dot(al, b_hi[n, k]))

    begun = set()

    def add_product(n, k, lo, hi):
        res = product(n, k, lo, hi).reshape(hi - lo, B, W)
        part[n, pl.ds(lo, hi - lo)] = part[n, pl.ds(lo, hi - lo)] + res if (n, lo) in begun else res
        begun.add((n, lo))

    def task(d, n):
        acc = jnp.zeros((B, W), F32)
        for k in range(NZ):
            acc = acc + product(n, k, POS[d], POS[d] + 1)
        part[n, POS[d]] = acc

    def step(n, rel):
        k = (z + rel) % NZ
        split_b(n, k)
        add_product(n, k, 0, NY if n == NS - 1 else NY - 1)

    def block(xr, zz):
        k = 2 * ((x + xr) % NX) + zz
        split_a(LATE_D, k)
        for n in range(NS):
            if n not in STEPPED:
                add_product(n, k, POS[LATE_D], POS[LATE_D] + 1)

    def put_var(n, prod):
        for j in (0, 1):
            vg[me8, pl.ds(2 * n + j, 1)] = prod[:, j * B:(j + 1) * B]

    for act in program:
        kind = act[0]
        if kind == "send":
            if act[1] == "VZ":
                for r in range(1, NZ):
                    column_sums("VZ", peer=at(dz=r)).start()
            elif act[1] == "VG":
                for r in range(1, 2 * NY):
                    column_sums("VG", peer=(z * 2 * NY + (me8 + r) % (2 * NY), x)).start()
            else:
                copy(act[1:], True).start()
        elif kind == "recv":
            if act[1] in ("VZ", "VG"):
                column_sums(act[1]).wait_recv()
            else:
                copy(act[1:], False).wait_recv()
        elif kind == "sent":
            if act[1] in ("VZ", "VG"):
                column_sums(act[1]).wait_send()
            else:
                copy(act[1:], True).wait_send()
        elif kind == "local":
            for cp in locals_:
                cp.start()
            for cp in locals_:
                cp.wait()
        elif kind == "prepA":
            prep_a(act[1])
        elif kind == "prepB":
            prep_b(act[1])
        elif kind == "task":
            task(act[1], act[2])
        elif kind == "step":
            step(act[1], act[2])
        elif kind == "block":
            block(act[1], act[2])
        elif kind == "y1":
            _, n, s = act
            i = 0 if s > 0 else 1
            half = pl.ds(i * (B // 2), B // 2)
            r1[i, n] = part[n, POS[s % NY], half] + r1[i, n]
        elif kind == "fin":
            n = act[1]
            out = part[n, 0] + (r2[0, n] + r2[1, n])
            cross[:, pl.ds(n * W, W)] = -out
            if n not in EARLY:
                put_var(n, jnp.sum(out * pbuf[n, 2 * z + c], axis=0, keepdims=True))
        elif kind == "vpart":
            n = act[1]
            prod = part[n, 0] * pbuf[n, 2 * z + c]
            for d in range(1, NY):
                prod = prod + part[n, POS[d]] * pv[EARLY.index(n), d]
            put_var(n, jnp.sum(prod, axis=0, keepdims=True))
        elif kind == "v2":
            total = vg[0]
            for i in range(1, 2 * NY):
                total = total + vg[i]
            vz[z] = total
        elif kind == "vend":
            total = vz[0]
            for i in range(1, NZ):
                total = total + vz[i]
            var[...] = diag[...] + total


def finish(cross, var, cross_out, var_out, sem):
    copies = [pltpu.make_async_copy(cross, cross_out, sem.at[0]), pltpu.make_async_copy(var, var_out, sem.at[1])]
    for copy in copies:
        copy.start()
    for copy in copies:
        copy.wait()


def body(sigma_anc, panel_hat, pattern, diag_inverse):
    program, slots = plan()[:2]
    sem_of = receive_slots(program)
    dma = pltpu.SemaphoreType.DMA
    vmem = pl.BlockSpec(memory_space=pltpu.VMEM)
    cross, var = pl.pallas_call(
        functools.partial(kernel, program, slots, sem_of),
        out_shape=(pltpu.VMEM((B, NS * W), F32), pltpu.VMEM((8, B), F32)),
        in_specs=[pl.BlockSpec(memory_space=pltpu.HBM)] * 4,
        out_specs=(vmem, vmem),
        scratch_shapes=[
            pltpu.VMEM((8, B), F32),
            pltpu.SMEM((NY * NZ * 2, NY * NZ * 2), jnp.int32),
            pltpu.VMEM((NS, 2 * NZ, B, W), F32),
            pltpu.VMEM((NY, NZ, B, W), F32),
            pltpu.VMEM((2, B, W), F32),
            pltpu.VMEM((NZ, NY * B, W), BF16),
            pltpu.VMEM((NZ, NY * B, W), BF16),
            pltpu.VMEM((NS, NZ, W, W), BF16),
            pltpu.VMEM((NS, NZ, W, W), BF16),
            pltpu.VMEM((NS, NY, B, W), F32),
            pltpu.VMEM((2, NS, B // 2, W), F32),
            pltpu.VMEM((2, NS, B, W), F32),
            pltpu.VMEM((len(EARLY), NY, B, W), F32),
            pltpu.VMEM((NZ, 8, B), F32),
            pltpu.VMEM((2 * NY, 8, B), F32),
            dma((SEND_POOL + 2,)),
            dma((max(sem_of.values()) + 1,)),
            dma((NS + 4,)),
        ],
        compiler_params=pltpu.CompilerParams(collective_id=0, has_side_effects=True, vmem_limit_bytes=56 * 1024 * 1024),
        name="selected_inverse",
    )(pattern, sigma_anc, panel_hat, diag_inverse.reshape(8, B))
    out, var = pl.pallas_call(
        finish,
        out_shape=(jax.ShapeDtypeStruct((B, NS * W), F32), jax.ShapeDtypeStruct((8, B), F32)),
        in_specs=[vmem, vmem],
        out_specs=(pl.BlockSpec(memory_space=pl.ANY),) * 2,
        scratch_shapes=[dma((2,))],
        name="finish",
    )(pltpu.with_memory_space_constraint(cross, pltpu.VMEM), pltpu.with_memory_space_constraint(var, pltpu.VMEM))
    return out, var.reshape(-1)


def solution(mesh):
    in_specs = (P("row", "col"), P("row", "col"), P(), P("col"))
    out_specs = (P("row", "col"), P("col"))
    return jax.shard_map(body, mesh=mesh, in_specs=in_specs, out_specs=out_specs, check_vma=False)
```

```python
import functools
import heapq

import jax
import jax.numpy as jnp
from jax import lax
from jax.experimental import pallas as pl
from jax.experimental.pallas import tpu as pltpu
from jax.sharding import PartitionSpec as P

MESH = pl.DeviceIdType.MESH
NX, NY, NZ = 4, 4, 8
B = 128
W = 256
NS = 4
F32, BF16 = jnp.float32, jnp.bfloat16

EARLY = (0, 1, 2, 3)
STEPPED = (2, 3)
LATE_D = 1
POS = (0, 3, 1, 2)
FAR = NZ // 2
SEND_POOL = 40
FIN = 2.6
Y_EXTRA = 0.4
AHEAD = 2
Y0 = -2.9
Y_SHARED = 25.0
X_WINDOW = 2
NEXT = (None, (1, 1), (2, 2), (1, 2))

LINK, LAT, CORE, CORE_LAT = 2.84, 2.1, 0.3, 1.0
T_ISSUE, T_PREP, T_TASK, T_SMALL, T_STEP, T_PART, T_BLOCK = 0.02, 0.035, 0.97, 0.05, 0.48, 0.36, 0.24
VZ_LAT, VG_LAT = 4.2, 3.0
D_ORDER = (0, 2, 3, 1)


def subs(s, h):
    first = 0 if s > 0 else 1
    return (first,) if h == FAR else (first, 1 - first)


def sgn(s):
    return "+" if s > 0 else "-"


def plan():
    program, arrivals, free, done_at = [], [], {}, {}
    clock = [0.0]
    got, seq, ends = set(), [0], {}

    def send(key, link, units=1.0):
        program.append(("send",) + key)
        clock[0] += T_ISSUE
        cost, lat = {"c": (CORE, CORE_LAT), "vz": (0.0, VZ_LAT), "vg": (0.0, VG_LAT)}.get(link, (LINK, LAT))
        start = max(clock[0], free.get(link, 0.0))
        if link == "vg":
            start = max([start] + [free.get(other, 0.0) for other in ("y+", "y-")])
        took = cost * units
        if link[0] == "y" and clock[0] > Y_SHARED:
            both = min(max(free.get("y+" if link == "y-" else "y-", 0.0) - start, 0.0), took)
            both = took if key[0] == "Y2" else both
            took = (took + both) / 2
        free[link] = start + took
        done_at[key] = ends[key] = free[link]
        seq[0] += 1
        heapq.heappush(arrivals, (free[link] + lat + (Y_EXTRA if key[0] in ("Y1", "Y2") else 0.0), seq[0], key))

    def pz(n, s, h, sub):
        send(("PZ", n, s, h, sub), "z" + sgn(s), 0.5)

    def start_slice(n, s):
        for sub in subs(s, 1):
            pz(n, s, 1, sub)

    order = {d: i for i, d in enumerate(D_ORDER)}
    held, under_way = [], {(0, 0): 2, (0, 1): 2}

    def forward_x():
        while held and len(under_way) < X_WINDOW:
            d, zz = min(held, key=lambda e: (order[e[0]], e[1]))
            if any(("own", e, f) not in got for e in D_ORDER[1:order[d]] for f in (0, 1)):
                return
            held.remove((d, zz))
            got.add(("own", d, zz))
            under_way[(d, zz)] = 2
            for s in (1, -1):
                send(("XS", d, zz, s, 1), "x" + sgn(s))

    def on(key):
        kind = key[0]
        if kind == "PZ":
            _, n, s, h, sub = key
            if h < FAR and sub in subs(s, h + 1):
                pz(n, s, h + 1, sub)
            if h == FAR:
                send(("PC", n, FAR, sub + 1), "c", 0.5)
            elif sub == subs(s, h)[1]:
                send(("PC", n, (-s * h) % NZ, 0), "c")
            for i, after in enumerate(NEXT[n + 1] if n + 1 < NS else ()):
                if (h, sub) == (after, subs(s, h)[0]):
                    pz(n + 1, s, 1, subs(s, 1)[i])
                    if s > 0 and i:
                        send(("PC", n + 1, 0, 0), "c")
        elif kind == "AR1":
            _, k, sub = key
            y = "y" + "+-"[k]
            send(("AR2", k, sub), y, 0.5)
            if not sub:
                return
            for zz in (0, 1):
                send(("AY", 1 - 2 * k, zz), y)
            for n in EARLY[:2]:
                send(("PY", n, 1 - 2 * k, 1), y)
        elif kind == "PY" and key[3] == 1:
            send(("PY", key[1], key[2], 2), "y" + sgn(key[2]), 0.5)
            if EARLY.index(key[1]) + 2 < len(EARLY):
                send(("PY", EARLY[EARLY.index(key[1]) + 2], key[2], 1), "y" + sgn(key[2]))
        elif kind in ("AY", "AR2"):
            if kind == "AR2" and not {("AR2", key[1], sub) for sub in (0, 1)} <= waited:
                return
            held.append(((-key[1]) % NY, key[2]) if kind == "AY" else (2, key[1]))
            forward_x()
        elif kind == "XS":
            _, d, zz, s, h = key
            if h == 1:
                send(("XS", d, zz, s, 2), "x" + sgn(s), 0.5)
            if h == 1:
                under_way[(d, zz)] -= 1
                if not under_way[(d, zz)]:
                    del under_way[(d, zz)]
                    forward_x()

    waited, times, came = set(), [], {}

    def receive(key):
        program.append(("recv",) + key)
        clock[0] += T_ISSUE
        waited.add(key)
        times.append((clock[0],) + key)

    def passes_on(key):
        if key[0] == "XS":
            return key[4] == 1
        if key[0] == "PY":
            return key[3] == 1
        return key[0] in ("PZ", "AR1", "AR2", "AY")

    for s in (1, -1):
        start_slice(0, s)
        for sub in (0, 1):
            send(("AR1", 0 if s > 0 else 1, sub), "y" + sgn(s), 0.5)
        send(("XS", 0, 0, s, 1), "x" + sgn(s))
    send(("PC", 0, 0, 0), "c")
    for s in (1, -1):
        send(("XS", 0, 1, s, 1), "x" + sgn(s))
    program.append(("local",))

    jobs = {}
    arrive = {n: {} for n in range(NS)}
    for n in range(NS):
        arrive[n][0] = {("PC", n, 0, 0)}
        for s in (1, -1):
            for h in range(1, FAR + 1):
                for sub in subs(s, h):
                    rel = (-s * h) % NZ
                    arrive[n].setdefault(rel, set()).update({("PZ", n, s, h, sub), ("PC", n, rel, sub + 1 if h == FAR else 0)})
    rows = {}
    for d in range(NY):
        need = {("XS", d, zz, s, h) for zz in (0, 1) for s in (1, -1) for h in (1, 2)}
        side = 1 if d == 3 else -1
        rows[d] = need | {0: set(), 2: {("AR2", k, sub) for k in (0, 1) for sub in (0, 1)}}.get(d, {("AY", side, 0), ("AY", side, 1)})
    ready_rows = {("prepA", d) for d in range(NY) if d != LATE_D}
    for d in range(NY):
        if d != LATE_D:
            jobs[("prepA", d)] = (-1.0, rows[d], T_PREP * 8)
    blocks = {("block", 0, zz): {("AY", -1, zz)} for zz in (0, 1)}
    blocks |= {("block", (-s) % NX, zz): {("XS", LATE_D, zz, s, 1)} for zz in (0, 1) for s in (1, -1)}
    blocks |= {("block", 2, zz): {("XS", LATE_D, zz, s, 2) for s in (1, -1)} for zz in (0, 1)}
    for job, need in blocks.items():
        jobs[job] = (-1.5, need | {("prepB", n) for n in range(NS) if n not in STEPPED}, T_BLOCK)
    for n in range(NS):
        whole = n == NS - 1
        if n in STEPPED:
            steps = {("step", n, rel) for rel in range(NZ)}
            for rel in range(NZ):
                jobs[("step", n, rel)] = (n - 0.5, arrive[n][rel] | ready_rows | (set(blocks) if whole else set()), T_STEP if whole else T_PART)
        else:
            jobs[("prepB", n)] = (-2.0, set().union(*arrive[n].values()), T_PREP * 16)
        done = {}
        for d in range(NY):
            if n not in STEPPED and d == LATE_D:
                done[d] = set(blocks)
            elif n in STEPPED and (whole or d != LATE_D):
                done[d] = steps
            else:
                done[d] = {("task", d, n)}
                need = set(blocks) | steps if n in STEPPED else {("prepA", d), ("prepB", n)}
                jobs[("task", d, n)] = (n + 0.1 * POS[d] - (1 if d == 2 else 0), need, T_TASK)
        everything = set().union(*done.values())
        first = ("vpart", n)
        if n in EARLY:
            jobs[first] = (-3.5, everything | {("PY", n, s, h) for s in (1, -1) for h in (1, 2)}, 0.1)
        jobs[("y2", n)] = (-3.0, done[2], 0.0)
        for s in (1, -1):
            after = {("y2", AHEAD)} if s % NY == LATE_D and n < AHEAD and n not in STEPPED else set()
            jobs[("y0", n, s)] = (Y0, done[s % NY] | after, 0.0)
            jobs[("y1", n, s)] = (-3.0, done[s % NY] | {("Y2", n, s)} | after, T_SMALL)
        jobs[("fin", n)] = (FIN, ({first} if n in EARLY else done[0]) | {("Y1", n, s, i) for s in (1, -1) for i in (0, 1)}, T_SMALL)
    jobs[("v1",)] = (-4.0, {("vpart", n) for n in EARLY} | {("fin", n) for n in range(NS) if n not in EARLY}, 0.0)
    jobs[("v2",)] = (-4.0, {("VG",)}, 0.05)
    jobs[("vend",)] = (-4.0, {("VZ",)}, 0.05)
    while jobs or arrivals:
        if arrivals and arrivals[0][0] <= clock[0]:
            when, _, key = heapq.heappop(arrivals)
            came[key] = when
            got.add(key)
            if passes_on(key):
                receive(key)
                on(key)
            continue
        ready = [(p, j) for j, (p, need, _) in jobs.items() if need <= got]
        if ready:
            job = min(ready, key=lambda r: (r[0], str(r[1])))[1]
            for key in sorted(jobs[job][1], key=str):
                if key[0].isupper() and key not in waited:
                    receive(key)
            program.append(job)
            times.append((clock[0],) + job)
            clock[0] += jobs.pop(job)[2]
            got.add(job)
            if job[0] == "y2":
                for s in (1, -1):
                    send(("Y2", job[1], s), "y" + sgn(s), 0.5)
            elif job[0] == "y1":
                send(("Y1", job[1], job[2], 1), "y" + sgn(job[2]), 0.5)
            elif job[0] == "y0":
                send(("Y1", job[1], job[2], 0), "y" + sgn(job[2]), 0.5)
            elif job[0] == "v1":
                send(("VG",), "vg")
            elif job[0] == "v2":
                send(("VZ",), "vz")
            continue
        old = [k for k in came if k not in waited and k[0] != "Y1" and came[k] + 2.0 < clock[0]]
        if old and arrivals and arrivals[0][0] > clock[0] + 0.1:
            receive(min(old, key=lambda k: (came[k], str(k))))
            continue
        late = sorted((t, k) for k, t in done_at.items() if t + 3.0 < clock[0])
        if late and arrivals and arrivals[0][0] > clock[0] + 0.1:
            program.append(("sent",) + late[0][1])
            del done_at[late[0][1]]
            clock[0] += 0.03
            continue
        clock[0] = max(clock[0], arrivals[0][0])

    final, slots, pool, flying = [], {}, list(range(SEND_POOL)), []
    for act in program:
        key = act[1:]
        if act[0] == "send" and key[0] not in ("VZ", "VG"):
            if not pool:
                old = min(flying, key=lambda k: (ends[k], str(k)))
                final.append(("sent",) + old)
                flying.remove(old)
                pool.append(slots[old])
            slots[key] = pool.pop(0)
            flying.append(key)
        if act[0] == "sent":
            if key not in flying:
                continue
            flying.remove(key)
            pool.append(slots[key])
        final.append(act)
    for key in flying + [("VZ",), ("VG",)]:
        final.append(("sent",) + key)
    return final, slots, clock[0], free, times


def receive_slots(program):
    at = {act: i for i, act in enumerate(program)}
    keys = [act[1:] for act in program if act[0] == "send"]

    def channel(key):
        if key[0] == "PC":
            return "c", 0
        if key[0] in ("AR1", "AR2"):
            return "y", 1 - 2 * key[1]
        return {"P": "z", "X": "x", "A": "y", "Y": "y"}["Y" if key[0] == "PY" else key[0][0]], key[{"PZ": 2, "XS": 3, "AY": 1, "PY": 2, "Y2": 2, "Y1": 2}[key[0]]]

    slots, users = {}, []
    for key in keys:
        if key[0] in ("VZ", "VG"):
            users.append(None)
            slots[key] = len(users) - 1
            continue
        axis, s = channel(key)
        back = [m for m in keys if m[0] not in ("VZ", "VG") and channel(m) == (axis, -s)]
        free = None
        for i, last in enumerate(users):
            if last is None or channel(last) != (axis, s):
                continue
            if any(at[("send",) + m] > at[("recv",) + last] and at[("recv",) + m] < at[("send",) + key] for m in back):
                free = i
                break
        if free is None:
            users.append(key)
            free = len(users) - 1
        users[free] = key
        slots[key] = free
    return slots


def kernel(program, slots, sem_of, pattern_hbm, sigma, panel, diag_hbm, cross, var, diag, pattern, pbuf, sbuf, relay, a_hi, a_lo, b_hi, b_lo, part, r1, r2,
           pv, vz, vg, send_sem, recv_sem, local_sem):
    row, x = lax.axis_index("row"), lax.axis_index("col")
    z, y, c = row // (2 * NY), (row // 2) % NY, row % 2
    flip_y = 1 - 2 * c

    def at(dx=0, dy=0, dz=0, flip=False):
        core = 1 - c if flip else c
        return ((((z + dz + NZ) % NZ) * NY + (y + flip_y * dy + NY) % NY) * 2 + core, (x + dx + NX) % NX)

    halves = [pl.ds(0, B // 2), pl.ds(B // 2, B // 2)]

    def lanes(start):
        return pl.ds(pl.multiple_of(start, W), W)

    def ends(key, sender):
        kind = key[0]
        if kind == "PZ":
            _, n, s, h, sub = key
            zs = (z - s * (h - 1 if sender else h) + NZ) % NZ
            dst = pbuf.at[n, 2 * zs + c, halves[sub]]
            src = panel.at[halves[sub], pl.ds(n * W, W)] if h == 1 else dst
            return src, dst, at(dz=s)
        if kind == "PC":
            _, n, rel, part_no = key
            zs = (z + rel) % NZ
            dst = pbuf.at[n, 2 * zs + (c if sender else 1 - c)]
            if part_no:
                dst = pbuf.at[n, 2 * zs + (c if sender else 1 - c), halves[part_no - 1]]
            src = panel.at[:, pl.ds(n * W, W)] if rel == 0 else dst
            return src, dst, at(flip=True)
        if kind == "AY":
            _, s, zz = key
            src = sigma.at[:, lanes(zz * NY * W + ((y + flip_y * s + NY) % NY) * W)]
            return src, sbuf.at[(-s) % NY, 2 * x + zz], at(dy=s)
        if kind == "AR1":
            _, k, sub = key
            src = sigma.at[halves[sub], lanes(k * NY * W + ((y + 2) % NY) * W)]
            return src, relay.at[k, halves[sub]], at(dy=1 - 2 * k)
        if kind == "AR2":
            _, k, sub = key
            return relay.at[k, halves[sub]], sbuf.at[2, 2 * x + k, halves[sub]], at(dy=1 - 2 * k)
        if kind == "XS":
            _, d, zz, s, h = key
            xs = (x - s * (h - 1 if sender else h) + NX) % NX
            dst = sbuf.at[d, 2 * xs + zz]
            if h == 2:
                dst = sbuf.at[d, 2 * xs + zz, halves[(1 - s) // 2]]
            src = sigma.at[:, lanes(zz * NY * W + y * W)] if d == 0 and h == 1 else dst
            return src, dst, at(dx=s)
        if kind == "PY":
            _, n, s, h = key
            e = EARLY.index(n)
            if h == 1:
                return panel.at[:, pl.ds(n * W, W)], pv.at[e, (-s) % NY], at(dy=s)
            half = halves[(1 - s) // 2]
            return pv.at[e, (-s) % NY, half], pv.at[e, 2, half], at(dy=s)
        if kind == "Y2":
            _, n, s = key
            i = 0 if s > 0 else 1
            return part.at[n, POS[2], pl.ds(i * (B // 2), B // 2)], r1.at[i, n], at(dy=s)
        _, n, s, i = key
        half = halves[(1 - s) // 2 if i else (1 + s) // 2]
        side = 0 if s > 0 else 1
        return r1.at[side, n] if i else part.at[n, POS[s % NY], half], r2.at[0 if s > 0 else 1, n, half], at(dy=s)

    def copy(key, sender):
        src, dst, target = ends(key, sender)
        return pltpu.make_async_remote_copy(
            src_ref=src if sender else dst, dst_ref=dst, send_sem=send_sem.at[slots[key]], recv_sem=recv_sem.at[sem_of[key]],
            device_id=target, device_id_type=MESH)

    def column_sums(kind, ref=None, peer=None):
        buf, mine = (vz, z) if kind == "VZ" else (vg, me8)
        ref = buf.at[pl.ds(0, 7)] if peer is None else buf.at[mine]
        i = 0 if kind == "VZ" else 1
        return pltpu.make_async_remote_copy(
            src_ref=ref, dst_ref=ref, send_sem=send_sem.at[SEND_POOL + i], recv_sem=recv_sem.at[sem_of[(kind,)]],
            device_id=at(dz=1) if peer is None else peer, device_id_type=MESH)

    me8 = row % (2 * NY)
    barrier = pltpu.get_barrier_semaphore()
    peers = [at(dx=1), at(dx=-1), at(dy=1), at(dy=-1), at(dz=1), at(dz=-1), at(flip=True)]
    for peer in peers:
        pl.semaphore_signal(barrier, inc=1, device_id=peer, device_id_type=MESH)
    locals_ = [pltpu.make_async_copy(panel.at[:, pl.ds(n * W, W)], pbuf.at[n, 2 * z + c], local_sem.at[n]) for n in range(NS)]
    locals_ += [pltpu.make_async_copy(sigma.at[:, lanes(zz * NY * W + y * W)], sbuf.at[0, 2 * x + zz], local_sem.at[NS + zz]) for zz in (0, 1)]
    locals_ += [pltpu.make_async_copy(pattern_hbm, pattern, local_sem.at[NS + 2])]
    locals_ += [pltpu.make_async_copy(diag_hbm, diag, local_sem.at[NS + 3])]
    pl.semaphore_wait(barrier, len(peers))

    def split_a(d, zk):
        rb = (z * NY + (y + flip_y * d + NY) % NY) * 2 + c
        cb = (zk * NY + y) * 2
        for j in (0, 1):
            m = pattern[rb, cb + j].astype(F32)
            v = sbuf[d, zk, :, pl.ds(j * B, B)] * m
            hi = v.astype(BF16)
            a_hi[zk, pl.ds(POS[d] * B, B), pl.ds(j * B, B)] = hi
            a_lo[zk, pl.ds(POS[d] * B, B), pl.ds(j * B, B)] = (v - hi.astype(F32)).astype(BF16)

    def prep_a(d):
        def one(zk, carry):
            split_a(d, zk)
            return carry

        lax.fori_loop(0, NZ, one, 0)

    def split_b(n, k):
        for j in (0, 1):
            p = pbuf[n, 2 * k + j]
            hi = p.astype(BF16)
            b_hi[n, k, pl.ds(j * B, B)] = hi
            b_lo[n, k, pl.ds(j * B, B)] = (p - hi.astype(F32)).astype(BF16)

    def prep_b(n):
        def one(k, carry):
            split_b(n, k)
            return carry

        lax.fori_loop(0, NZ, one, 0)

    dot = functools.partial(jnp.dot, preferred_element_type=F32)

    def product(n, k, lo, hi):
        ah, al = a_hi[k, pl.ds(lo * B, (hi - lo) * B)], a_lo[k, pl.ds(lo * B, (hi - lo) * B)]
        return dot(ah, b_hi[n, k]) + (dot(ah, b_lo[n, k]) + dot(al, b_hi[n, k]))

    begun = set()

    def add_product(n, k, lo, hi):
        res = product(n, k, lo, hi).reshape(hi - lo, B, W)
        part[n, pl.ds(lo, hi - lo)] = part[n, pl.ds(lo, hi - lo)] + res if (n, lo) in begun else res
        begun.add((n, lo))

    def task(d, n):
        acc = jnp.zeros((B, W), F32)
        for k in range(NZ):
            acc = acc + product(n, k, POS[d], POS[d] + 1)
        part[n, POS[d]] = acc

    def step(n, rel):
        k = (z + rel) % NZ
        split_b(n, k)
        add_product(n, k, 0, NY if n == NS - 1 else NY - 1)

    def block(xr, zz):
        k = 2 * ((x + xr) % NX) + zz
        split_a(LATE_D, k)
        for n in range(NS):
            if n not in STEPPED:
                add_product(n, k, POS[LATE_D], POS[LATE_D] + 1)

    def put_var(n, prod):
        for j in (0, 1):
            vg[me8, pl.ds(2 * n + j, 1)] = prod[:, j * B:(j + 1) * B]

    for act in program:
        kind = act[0]
        if kind == "send":
            if act[1] == "VZ":
                for r in range(1, NZ):
                    column_sums("VZ", peer=at(dz=r)).start()
            elif act[1] == "VG":
                for r in range(1, 2 * NY):
                    column_sums("VG", peer=(z * 2 * NY + (me8 + r) % (2 * NY), x)).start()
            else:
                copy(act[1:], True).start()
        elif kind == "recv":
            if act[1] in ("VZ", "VG"):
                column_sums(act[1]).wait_recv()
            else:
                copy(act[1:], False).wait_recv()
        elif kind == "sent":
            if act[1] in ("VZ", "VG"):
                column_sums(act[1]).wait_send()
            else:
                copy(act[1:], True).wait_send()
        elif kind == "local":
            for cp in locals_:
                cp.start()
            for cp in locals_:
                cp.wait()
        elif kind == "prepA":
            prep_a(act[1])
        elif kind == "prepB":
            prep_b(act[1])
        elif kind == "task":
            task(act[1], act[2])
        elif kind == "step":
            step(act[1], act[2])
        elif kind == "block":
            block(act[1], act[2])
        elif kind == "y1":
            _, n, s = act
            i = 0 if s > 0 else 1
            half = pl.ds(i * (B // 2), B // 2)
            r1[i, n] = part[n, POS[s % NY], half] + r1[i, n]
        elif kind == "fin":
            n = act[1]
            out = part[n, 0] + (r2[0, n] + r2[1, n])
            cross[:, pl.ds(n * W, W)] = -out
            if n not in EARLY:
                put_var(n, jnp.sum(out * pbuf[n, 2 * z + c], axis=0, keepdims=True))
        elif kind == "vpart":
            n = act[1]
            prod = part[n, 0] * pbuf[n, 2 * z + c]
            for d in range(1, NY):
                prod = prod + part[n, POS[d]] * pv[EARLY.index(n), d]
            put_var(n, jnp.sum(prod, axis=0, keepdims=True))
        elif kind == "v2":
            total = vg[0]
            for i in range(1, 2 * NY):
                total = total + vg[i]
            vz[z] = total
        elif kind == "vend":
            total = vz[0]
            for i in range(1, NZ):
                total = total + vz[i]
            var[...] = diag[...] + total


def finish(cross, var, cross_out, var_out, sem):
    copies = [pltpu.make_async_copy(cross, cross_out, sem.at[0]), pltpu.make_async_copy(var, var_out, sem.at[1])]
    for copy in copies:
        copy.start()
    for copy in copies:
        copy.wait()


def body(sigma_anc, panel_hat, pattern, diag_inverse):
    program, slots = plan()[:2]
    sem_of = receive_slots(program)
    dma = pltpu.SemaphoreType.DMA
    vmem = pl.BlockSpec(memory_space=pltpu.VMEM)
    cross, var = pl.pallas_call(
        functools.partial(kernel, program, slots, sem_of),
        out_shape=(pltpu.VMEM((B, NS * W), F32), pltpu.VMEM((8, B), F32)),
        in_specs=[pl.BlockSpec(memory_space=pltpu.HBM)] * 4,
        out_specs=(vmem, vmem),
        scratch_shapes=[
            pltpu.VMEM((8, B), F32),
            pltpu.SMEM((NY * NZ * 2, NY * NZ * 2), jnp.int32),
            pltpu.VMEM((NS, 2 * NZ, B, W), F32),
            pltpu.VMEM((NY, NZ, B, W), F32),
            pltpu.VMEM((2, B, W), F32),
            pltpu.VMEM((NZ, NY * B, W), BF16),
            pltpu.VMEM((NZ, NY * B, W), BF16),
            pltpu.VMEM((NS, NZ, W, W), BF16),
            pltpu.VMEM((NS, NZ, W, W), BF16),
            pltpu.VMEM((NS, NY, B, W), F32),
            pltpu.VMEM((2, NS, B // 2, W), F32),
            pltpu.VMEM((2, NS, B, W), F32),
            pltpu.VMEM((len(EARLY), NY, B, W), F32),
            pltpu.VMEM((NZ, 8, B), F32),
            pltpu.VMEM((2 * NY, 8, B), F32),
            dma((SEND_POOL + 2,)),
            dma((max(sem_of.values()) + 1,)),
            dma((NS + 4,)),
        ],
        compiler_params=pltpu.CompilerParams(collective_id=0, has_side_effects=True, vmem_limit_bytes=56 * 1024 * 1024),
        name="selected_inverse",
    )(pattern, sigma_anc, panel_hat, diag_inverse.reshape(8, B))
    out, var = pl.pallas_call(
        finish,
        out_shape=(jax.ShapeDtypeStruct((B, NS * W), F32), jax.ShapeDtypeStruct((8, B), F32)),
        in_specs=[vmem, vmem],
        out_specs=(pl.BlockSpec(memory_space=pl.ANY),) * 2,
        scratch_shapes=[dma((2,))],
        name="finish",
    )(pltpu.with_memory_space_constraint(cross, pltpu.VMEM), pltpu.with_memory_space_constraint(var, pltpu.VMEM))
    return out, var.reshape(-1)


def solution(mesh):
    in_specs = (P("row", "col"), P("row", "col"), P(), P("col"))
    out_specs = (P("row", "col"), P("col"))
    return jax.shard_map(body, mesh=mesh, in_specs=in_specs, out_specs=out_specs, check_vma=False)
```

```python
import functools
import heapq

import jax
import jax.numpy as jnp
from jax import lax
from jax.experimental import pallas as pl
from jax.experimental.pallas import tpu as pltpu
from jax.sharding import PartitionSpec as P

MESH = pl.DeviceIdType.MESH
NX, NY, NZ = 4, 4, 8
B = 128
W = 256
NS = 4
F32, BF16 = jnp.float32, jnp.bfloat16

EARLY = (0, 1, 2, 3)
LAST = NS - 1
STEPPED = (2, 3)
LATE_D = 1
POS = (0, 3, 1, 2)
FAR = NZ // 2
SEND_POOL = 24
FIN = 2.6
Y_EXTRA = 0.4
AHEAD = 0
Y0 = -2.9
Y_SHARED = 25.0
X_WINDOW = 2
NEXT = (None, (1, 1), (2, 2), (1, 2))

LINK, LAT, CORE, CORE_LAT = 2.84, 2.1, 0.3, 1.0
T_ISSUE, T_PREP, T_TASK, T_SMALL, T_STEP, T_PART, T_BLOCK = 0.02, 0.035, 0.97, 0.05, 0.48, 0.36, 0.24
VZ_LAT, VG_LAT = 4.2, 3.0
D_ORDER = (0, 2, 3, 1)


def subs(s, h):
    first = 0 if s > 0 else 1
    return (first,) if h == FAR else (first, 1 - first)


def sgn(s):
    return "+" if s > 0 else "-"


def plan():
    program, arrivals, free, done_at = [], [], {}, {}
    clock = [0.0]
    got, seq, ends = set(), [0], {}

    def send(key, link, units=1.0):
        program.append(("send",) + key)
        clock[0] += T_ISSUE
        cost, lat = {"c": (CORE, CORE_LAT), "vz": (0.0, VZ_LAT), "vg": (0.0, VG_LAT)}.get(link, (LINK, LAT))
        start = max(clock[0], free.get(link, 0.0))
        if link == "vg":
            start = max([start] + [free.get(other, 0.0) for other in ("y+", "y-")])
        took = cost * units
        if link[0] == "y" and clock[0] > Y_SHARED:
            both = min(max(free.get("y+" if link == "y-" else "y-", 0.0) - start, 0.0), took)
            both = took if key[0] == "Y2" else both
            took = (took + both) / 2
        free[link] = start + took
        done_at[key] = ends[key] = free[link]
        seq[0] += 1
        heapq.heappush(arrivals, (free[link] + lat + (Y_EXTRA if key[0] in ("Y1", "Y2") else 0.0), seq[0], key))

    def pz(n, s, h, sub):
        send(("PZ", n, s, h, sub), "z" + sgn(s), 0.5)

    def start_slice(n, s):
        for sub in subs(s, 1):
            pz(n, s, 1, sub)

    order = {d: i for i, d in enumerate(D_ORDER)}
    held, under_way = [], {(0, 0): 2, (0, 1): 2}

    def forward_x():
        while held and len(under_way) < X_WINDOW:
            d, zz = min(held, key=lambda e: (order[e[0]], e[1]))
            if any(("own", e, f) not in got for e in D_ORDER[1:order[d]] for f in (0, 1)):
                return
            held.remove((d, zz))
            got.add(("own", d, zz))
            under_way[(d, zz)] = 2
            for s in (1, -1):
                send(("XS", d, zz, s, 1), "x" + sgn(s))

    def on(key):
        kind = key[0]
        if kind == "PZ":
            _, n, s, h, sub = key
            if h < FAR and sub in subs(s, h + 1):
                pz(n, s, h + 1, sub)
            if h == FAR:
                send(("PC", n, FAR, sub + 1), "c", 0.5)
            elif sub == subs(s, h)[1]:
                send(("PC", n, (-s * h) % NZ, 0), "c")
            for i, after in enumerate(NEXT[n + 1] if n + 1 < NS else ()):
                if (h, sub) == (after, subs(s, h)[0]):
                    pz(n + 1, s, 1, subs(s, 1)[i])
                    if s > 0 and i:
                        send(("PC", n + 1, 0, 0), "c")
        elif kind == "AR1":
            _, k, sub = key
            y = "y" + "+-"[k]
            send(("AR2", k, sub), y, 0.5)
            if not sub:
                return
            for zz in (0, 1):
                send(("AY", 1 - 2 * k, zz), y)
            for n in EARLY[:2]:
                send(("PY", n, 1 - 2 * k, 1), y)
        elif kind == "PY" and key[3] == 1:
            send(("PY", key[1], key[2], 2), "y" + sgn(key[2]), 0.5)
            if EARLY.index(key[1]) + 2 < len(EARLY):
                send(("PY", EARLY[EARLY.index(key[1]) + 2], key[2], 1), "y" + sgn(key[2]))
        elif kind in ("AY", "AR2"):
            if kind == "AR2" and not {("AR2", key[1], sub) for sub in (0, 1)} <= waited:
                return
            held.append(((-key[1]) % NY, key[2]) if kind == "AY" else (2, key[1]))
            forward_x()
        elif kind == "XS":
            _, d, zz, s, h = key
            if h == 1:
                send(("XS", d, zz, s, 2), "x" + sgn(s), 0.5)
            if h == 1:
                under_way[(d, zz)] -= 1
                if not under_way[(d, zz)]:
                    del under_way[(d, zz)]
                    forward_x()

    waited, times, came = set(), [], {}

    def receive(key):
        program.append(("recv",) + key)
        clock[0] += T_ISSUE
        waited.add(key)
        times.append((clock[0],) + key)

    def passes_on(key):
        if key[0] == "XS":
            return key[4] == 1
        if key[0] == "PY":
            return key[3] == 1
        return key[0] in ("PZ", "AR1", "AR2", "AY")

    for s in (1, -1):
        start_slice(0, s)
        for sub in (0, 1):
            send(("AR1", 0 if s > 0 else 1, sub), "y" + sgn(s), 0.5)
        send(("XS", 0, 0, s, 1), "x" + sgn(s))
    send(("PC", 0, 0, 0), "c")
    for s in (1, -1):
        send(("XS", 0, 1, s, 1), "x" + sgn(s))
    program.append(("local",))

    jobs = {}
    arrive = {n: {} for n in range(NS)}
    for n in range(NS):
        arrive[n][0] = {("PC", n, 0, 0)}
        for s in (1, -1):
            for h in range(1, FAR + 1):
                for sub in subs(s, h):
                    rel = (-s * h) % NZ
                    arrive[n].setdefault(rel, set()).update({("PZ", n, s, h, sub), ("PC", n, rel, sub + 1 if h == FAR else 0)})
    rows = {}
    for d in range(NY):
        need = {("XS", d, zz, s, h) for zz in (0, 1) for s in (1, -1) for h in (1, 2)}
        side = 1 if d == 3 else -1
        rows[d] = need | {0: set(), 2: {("AR2", k, sub) for k in (0, 1) for sub in (0, 1)}}.get(d, {("AY", side, 0), ("AY", side, 1)})
    ready_rows = {("prepA", d) for d in range(NY) if d != LATE_D}
    for d in range(NY):
        if d != LATE_D:
            jobs[("prepA", d)] = (-1.0, rows[d], T_PREP * 8)
    blocks = {("block", 0, zz): {("AY", -1, zz)} for zz in (0, 1)}
    blocks |= {("block", (-s) % NX, zz): {("XS", LATE_D, zz, s, 1)} for zz in (0, 1) for s in (1, -1)}
    blocks |= {("block", 2, zz): {("XS", LATE_D, zz, s, 2) for s in (1, -1)} for zz in (0, 1)}
    for job, need in blocks.items():
        jobs[job] = (-1.5, need | {("prepB", n) for n in range(NS) if n not in STEPPED}, T_BLOCK)
    for n in range(NS):
        whole = n == NS - 1
        if n in STEPPED:
            steps = {("step", n, rel) for rel in range(NZ)}
            for rel in range(NZ):
                jobs[("step", n, rel)] = (n - 0.5, arrive[n][rel] | ready_rows | (set(blocks) if whole else set()), T_STEP if whole else T_PART)
        else:
            jobs[("prepB", n)] = (-2.0, set().union(*arrive[n].values()), T_PREP * 16)
        done = {}
        for d in range(NY):
            if n not in STEPPED and d == LATE_D:
                done[d] = set(blocks)
            elif n in STEPPED and (whole or d != LATE_D):
                done[d] = steps
            else:
                done[d] = {("task", d, n)}
                need = set(blocks) | steps if n in STEPPED else {("prepA", d), ("prepB", n)}
                jobs[("task", d, n)] = (n + 0.1 * POS[d] - (1 if d == 2 else 0), need, T_TASK)
        everything = set().union(*done.values())
        first = ("vpart", n)
        if n in EARLY:
            jobs[first] = (-3.5, everything | {("PY", n, s, h) for s in (1, -1) for h in (1, 2)}, 0.1)
        jobs[("y2", n)] = (-3.0, done[2], 0.0)
        for s in (1, -1):
            after = {("y2", AHEAD)} if s % NY == LATE_D and n < AHEAD and n not in STEPPED else set()
            jobs[("y0", n, s)] = (Y0, done[s % NY] | after, 0.0)
            jobs[("y1", n, s)] = (-3.0, done[s % NY] | {("Y2", n, s)} | after, T_SMALL)
        jobs[("fin", n)] = (FIN, ({first} if n in EARLY else done[0]) | {("Y1", n, s, i) for s in (1, -1) for i in (0, 1)} | {("vpart", LAST)}, T_SMALL)
    jobs[("v1",)] = (-4.0, {("vpart", n) for n in EARLY} | {("fin", n) for n in range(NS) if n not in EARLY}, 0.0)
    jobs[("v2",)] = (-4.0, {("VG",)}, 0.05)
    jobs[("vend",)] = (-4.0, {("VZ",)}, 0.05)
    while jobs or arrivals:
        if arrivals and arrivals[0][0] <= clock[0]:
            when, _, key = heapq.heappop(arrivals)
            came[key] = when
            got.add(key)
            if passes_on(key):
                receive(key)
                on(key)
            continue
        ready = [(p, j) for j, (p, need, _) in jobs.items() if need <= got]
        if ready:
            job = min(ready, key=lambda r: (r[0], str(r[1])))[1]
            for key in sorted(jobs[job][1], key=str):
                if key[0].isupper() and key not in waited:
                    receive(key)
            program.append(job)
            times.append((clock[0],) + job)
            clock[0] += jobs.pop(job)[2]
            got.add(job)
            if job[0] == "y2":
                for s in (1, -1):
                    send(("Y2", job[1], s), "y" + sgn(s), 0.5)
            elif job[0] == "y1":
                send(("Y1", job[1], job[2], 1), "y" + sgn(job[2]), 0.5)
            elif job[0] == "y0":
                send(("Y1", job[1], job[2], 0), "y" + sgn(job[2]), 0.5)
            elif job[0] == "v1":
                send(("VG",), "vg")
            elif job[0] == "v2":
                send(("VZ",), "vz")
            continue
        old = [k for k in came if k not in waited and k[0] != "Y1" and came[k] + 2.0 < clock[0]]
        if old and arrivals and arrivals[0][0] > clock[0] + 0.1:
            receive(min(old, key=lambda k: (came[k], str(k))))
            continue
        late = sorted((t, k) for k, t in done_at.items() if t + 3.0 < clock[0])
        if late and arrivals and arrivals[0][0] > clock[0] + 0.1:
            program.append(("sent",) + late[0][1])
            del done_at[late[0][1]]
            clock[0] += 0.03
            continue
        clock[0] = max(clock[0], arrivals[0][0])

    final, slots, pool, flying = [], {}, list(range(SEND_POOL)), []
    for act in program:
        key = act[1:]
        if act[0] == "send" and key[0] not in ("VZ", "VG"):
            if not pool:
                old = min(flying, key=lambda k: (ends[k], str(k)))
                final.append(("sent",) + old)
                flying.remove(old)
                pool.append(slots[old])
            slots[key] = pool.pop(0)
            flying.append(key)
        if act[0] == "sent":
            if key not in flying:
                continue
            flying.remove(key)
            pool.append(slots[key])
        final.append(act)
    for key in flying + [("VZ",), ("VG",)]:
        final.append(("sent",) + key)
    return final, slots, clock[0], free, times


def receive_slots(program):
    at = {act: i for i, act in enumerate(program)}
    keys = [act[1:] for act in program if act[0] == "send"]

    def channel(key):
        if key[0] == "PC":
            return "c", 0
        if key[0] in ("AR1", "AR2"):
            return "y", 1 - 2 * key[1]
        return {"P": "z", "X": "x", "A": "y", "Y": "y"}["Y" if key[0] == "PY" else key[0][0]], key[{"PZ": 2, "XS": 3, "AY": 1, "PY": 2, "Y2": 2, "Y1": 2}[key[0]]]

    slots, users = {}, []
    for key in keys:
        if key[0] in ("VZ", "VG"):
            users.append(None)
            slots[key] = len(users) - 1
            continue
        axis, s = channel(key)
        back = [m for m in keys if m[0] not in ("VZ", "VG") and channel(m) == (axis, -s)]
        free = None
        for i, last in enumerate(users):
            if last is None:
                continue
            if any(at[("send",) + m] > at[("recv",) + last] and at[("recv",) + m] < at[("send",) + key] for m in back):
                free = i
                break
        if free is None:
            users.append(key)
            free = len(users) - 1
        users[free] = key
        slots[key] = free
    return slots


def kernel(program, slots, sem_of, pattern_hbm, sigma, panel, diag_hbm, cross, var, diag, pattern, pbuf, sbuf, relay, a_hi, a_lo, b_hi, b_lo, part, r1, r2,
           pv, vz, vg, send_sem, recv_sem, local_sem):
    row, x = lax.axis_index("row"), lax.axis_index("col")
    z, y, c = row // (2 * NY), (row // 2) % NY, row % 2
    flip_y = 1 - 2 * c

    def at(dx=0, dy=0, dz=0, flip=False):
        core = 1 - c if flip else c
        return ((((z + dz + NZ) % NZ) * NY + (y + flip_y * dy + NY) % NY) * 2 + core, (x + dx + NX) % NX)

    halves = [pl.ds(0, B // 2), pl.ds(B // 2, B // 2)]

    def lanes(start):
        return pl.ds(pl.multiple_of(start, W), W)

    def ends(key, sender):
        kind = key[0]
        if kind == "PZ":
            _, n, s, h, sub = key
            zs = (z - s * (h - 1 if sender else h) + NZ) % NZ
            dst = pbuf.at[n, 2 * zs + c, halves[sub]]
            src = panel.at[halves[sub], pl.ds(n * W, W)] if h == 1 else dst
            return src, dst, at(dz=s)
        if kind == "PC":
            _, n, rel, part_no = key
            zs = (z + rel) % NZ
            dst = pbuf.at[n, 2 * zs + (c if sender else 1 - c)]
            if part_no:
                dst = pbuf.at[n, 2 * zs + (c if sender else 1 - c), halves[part_no - 1]]
            src = panel.at[:, pl.ds(n * W, W)] if rel == 0 else dst
            return src, dst, at(flip=True)
        if kind == "AY":
            _, s, zz = key
            src = sigma.at[:, lanes(zz * NY * W + ((y + flip_y * s + NY) % NY) * W)]
            return src, sbuf.at[(-s) % NY, 2 * x + zz], at(dy=s)
        if kind == "AR1":
            _, k, sub = key
            src = sigma.at[halves[sub], lanes(k * NY * W + ((y + 2) % NY) * W)]
            return src, relay.at[k, halves[sub]], at(dy=1 - 2 * k)
        if kind == "AR2":
            _, k, sub = key
            return relay.at[k, halves[sub]], sbuf.at[2, 2 * x + k, halves[sub]], at(dy=1 - 2 * k)
        if kind == "XS":
            _, d, zz, s, h = key
            xs = (x - s * (h - 1 if sender else h) + NX) % NX
            dst = sbuf.at[d, 2 * xs + zz]
            if h == 2:
                dst = sbuf.at[d, 2 * xs + zz, halves[(1 - s) // 2]]
            src = sigma.at[:, lanes(zz * NY * W + y * W)] if d == 0 and h == 1 else dst
            return src, dst, at(dx=s)
        if kind == "PY":
            _, n, s, h = key
            e = EARLY.index(n)
            if h == 1:
                return panel.at[:, pl.ds(n * W, W)], pv.at[e, (-s) % NY], at(dy=s)
            half = halves[(1 - s) // 2]
            return pv.at[e, (-s) % NY, half], pv.at[e, 2, half], at(dy=s)
        if kind == "Y2":
            _, n, s = key
            i = 0 if s > 0 else 1
            return part.at[n, POS[2], pl.ds(i * (B // 2), B // 2)], r1.at[i, n], at(dy=s)
        _, n, s, i = key
        half = halves[(1 - s) // 2 if i else (1 + s) // 2]
        side = 0 if s > 0 else 1
        return r1.at[side, n] if i else part.at[n, POS[s % NY], half], r2.at[0 if s > 0 else 1, n, half], at(dy=s)

    def copy(key, sender):
        src, dst, target = ends(key, sender)
        return pltpu.make_async_remote_copy(
            src_ref=src if sender else dst, dst_ref=dst, send_sem=send_sem.at[slots[key]], recv_sem=recv_sem.at[sem_of[key]],
            device_id=target, device_id_type=MESH)

    def column_sums(kind, ref=None, peer=None):
        buf, mine = (vz, z) if kind == "VZ" else (vg, me8)
        ref = buf.at[pl.ds(0, 7)] if peer is None else buf.at[mine]
        i = 0 if kind == "VZ" else 1
        return pltpu.make_async_remote_copy(
            src_ref=ref, dst_ref=ref, send_sem=send_sem.at[SEND_POOL + i], recv_sem=recv_sem.at[sem_of[(kind,)]],
            device_id=at(dz=1) if peer is None else peer, device_id_type=MESH)

    me8 = row % (2 * NY)
    barrier = pltpu.get_barrier_semaphore()
    peers = [at(dx=1), at(dx=-1), at(dy=1), at(dy=-1), at(dz=1), at(dz=-1), at(flip=True)]
    for peer in peers:
        pl.semaphore_signal(barrier, inc=1, device_id=peer, device_id_type=MESH)
    locals_ = [pltpu.make_async_copy(panel.at[:, pl.ds(n * W, W)], pbuf.at[n, 2 * z + c], local_sem.at[n]) for n in range(NS)]
    locals_ += [pltpu.make_async_copy(sigma.at[:, lanes(zz * NY * W + y * W)], sbuf.at[0, 2 * x + zz], local_sem.at[NS + zz]) for zz in (0, 1)]
    locals_ += [pltpu.make_async_copy(pattern_hbm, pattern, local_sem.at[NS + 2])]
    locals_ += [pltpu.make_async_copy(diag_hbm, diag, local_sem.at[NS + 3])]
    pl.semaphore_wait(barrier, len(peers))

    def split_a(d, zk):
        rb = (z * NY + (y + flip_y * d + NY) % NY) * 2 + c
        cb = (zk * NY + y) * 2
        for j in (0, 1):
            m = pattern[rb, cb + j].astype(F32)
            v = sbuf[d, zk, :, pl.ds(j * B, B)] * m
            hi = v.astype(BF16)
            a_hi[zk, pl.ds(POS[d] * B, B), pl.ds(j * B, B)] = hi
            a_lo[zk, pl.ds(POS[d] * B, B), pl.ds(j * B, B)] = (v - hi.astype(F32)).astype(BF16)

    def prep_a(d):
        def one(zk, carry):
            split_a(d, zk)
            return carry

        lax.fori_loop(0, NZ, one, 0)

    def split_b(n, k):
        for j in (0, 1):
            p = pbuf[n, 2 * k + j]
            hi = p.astype(BF16)
            b_hi[n, k, pl.ds(j * B, B)] = hi
            b_lo[n, k, pl.ds(j * B, B)] = (p - hi.astype(F32)).astype(BF16)

    def prep_b(n):
        def one(k, carry):
            split_b(n, k)
            return carry

        lax.fori_loop(0, NZ, one, 0)

    dot = functools.partial(jnp.dot, preferred_element_type=F32)

    def product(n, k, lo, hi):
        ah, al = a_hi[k, pl.ds(lo * B, (hi - lo) * B)], a_lo[k, pl.ds(lo * B, (hi - lo) * B)]
        return dot(ah, b_hi[n, k]) + (dot(ah, b_lo[n, k]) + dot(al, b_hi[n, k]))

    begun = set()

    def add_product(n, k, lo, hi):
        res = product(n, k, lo, hi).reshape(hi - lo, B, W)
        part[n, pl.ds(lo, hi - lo)] = part[n, pl.ds(lo, hi - lo)] + res if (n, lo) in begun else res
        begun.add((n, lo))

    def task(d, n):
        acc = jnp.zeros((B, W), F32)
        for k in range(NZ):
            acc = acc + product(n, k, POS[d], POS[d] + 1)
        part[n, POS[d]] = acc

    def step(n, rel):
        k = (z + rel) % NZ
        split_b(n, k)
        add_product(n, k, 0, NY if n == NS - 1 else NY - 1)

    def block(xr, zz):
        k = 2 * ((x + xr) % NX) + zz
        split_a(LATE_D, k)
        for n in range(NS):
            if n not in STEPPED:
                add_product(n, k, POS[LATE_D], POS[LATE_D] + 1)

    def put_var(n, prod):
        for j in (0, 1):
            vg[me8, pl.ds(2 * n + j, 1)] = prod[:, j * B:(j + 1) * B]

    for act in program:
        kind = act[0]
        if kind == "send":
            if act[1] == "VZ":
                for r in range(1, NZ):
                    column_sums("VZ", peer=at(dz=r)).start()
            elif act[1] == "VG":
                for r in range(1, 2 * NY):
                    column_sums("VG", peer=(z * 2 * NY + (me8 + r) % (2 * NY), x)).start()
            else:
                copy(act[1:], True).start()
        elif kind == "recv":
            if act[1] in ("VZ", "VG"):
                column_sums(act[1]).wait_recv()
            else:
                copy(act[1:], False).wait_recv()
        elif kind == "sent":
            if act[1] in ("VZ", "VG"):
                column_sums(act[1]).wait_send()
            else:
                copy(act[1:], True).wait_send()
        elif kind == "local":
            for cp in locals_:
                cp.start()
            for cp in locals_:
                cp.wait()
        elif kind == "prepA":
            prep_a(act[1])
        elif kind == "prepB":
            prep_b(act[1])
        elif kind == "task":
            task(act[1], act[2])
        elif kind == "step":
            step(act[1], act[2])
        elif kind == "block":
            block(act[1], act[2])
        elif kind == "y1":
            _, n, s = act
            i = 0 if s > 0 else 1
            half = pl.ds(i * (B // 2), B // 2)
            r1[i, n] = part[n, POS[s % NY], half] + r1[i, n]
        elif kind == "fin":
            n = act[1]
            out = part[n, 0] + (r2[0, n] + r2[1, n])
            cross[:, pl.ds(n * W, W)] = -out
            if n not in EARLY:
                put_var(n, jnp.sum(out * pbuf[n, 2 * z + c], axis=0, keepdims=True))
        elif kind == "vpart":
            n = act[1]
            prod = part[n, 0] * pbuf[n, 2 * z + c]
            for d in range(1, NY):
                prod = prod + part[n, POS[d]] * pv[EARLY.index(n), d]
            put_var(n, jnp.sum(prod, axis=0, keepdims=True))
        elif kind == "v2":
            total = vg[0]
            for i in range(1, 2 * NY):
                total = total + vg[i]
            vz[z] = total
        elif kind == "vend":
            total = vz[0]
            for i in range(1, NZ):
                total = total + vz[i]
            var[...] = diag[...] + total


def finish(cross, var, cross_out, var_out, sem):
    copies = [pltpu.make_async_copy(cross, cross_out, sem.at[0]), pltpu.make_async_copy(var, var_out, sem.at[1])]
    for copy in copies:
        copy.start()
    for copy in copies:
        copy.wait()


def body(sigma_anc, panel_hat, pattern, diag_inverse):
    program, slots = plan()[:2]
    sem_of = receive_slots(program)
    dma = pltpu.SemaphoreType.DMA
    vmem = pl.BlockSpec(memory_space=pltpu.VMEM)
    cross, var = pl.pallas_call(
        functools.partial(kernel, program, slots, sem_of),
        out_shape=(pltpu.VMEM((B, NS * W), F32), pltpu.VMEM((8, B), F32)),
        in_specs=[pl.BlockSpec(memory_space=pltpu.HBM)] * 4,
        out_specs=(vmem, vmem),
        scratch_shapes=[
            pltpu.VMEM((8, B), F32),
            pltpu.SMEM((NY * NZ * 2, NY * NZ * 2), jnp.int32),
            pltpu.VMEM((NS, 2 * NZ, B, W), F32),
            pltpu.VMEM((NY, NZ, B, W), F32),
            pltpu.VMEM((2, B, W), F32),
            pltpu.VMEM((NZ, NY * B, W), BF16),
            pltpu.VMEM((NZ, NY * B, W), BF16),
            pltpu.VMEM((NS, NZ, W, W), BF16),
            pltpu.VMEM((NS, NZ, W, W), BF16),
            pltpu.VMEM((NS, NY, B, W), F32),
            pltpu.VMEM((2, NS, B // 2, W), F32),
            pltpu.VMEM((2, NS, B, W), F32),
            pltpu.VMEM((len(EARLY), NY, B, W), F32),
            pltpu.VMEM((NZ, 8, B), F32),
            pltpu.VMEM((2 * NY, 8, B), F32),
            dma((SEND_POOL + 2,)),
            dma((max(sem_of.values()) + 1,)),
            dma((NS + 4,)),
        ],
        compiler_params=pltpu.CompilerParams(collective_id=0, has_side_effects=True, vmem_limit_bytes=56 * 1024 * 1024),
        name="selected_inverse",
    )(pattern, sigma_anc, panel_hat, diag_inverse.reshape(8, B))
    out, var = pl.pallas_call(
        finish,
        out_shape=(jax.ShapeDtypeStruct((B, NS * W), F32), jax.ShapeDtypeStruct((8, B), F32)),
        in_specs=[vmem, vmem],
        out_specs=(pl.BlockSpec(memory_space=pl.ANY),) * 2,
        scratch_shapes=[dma((2,))],
        name="finish",
    )(pltpu.with_memory_space_constraint(cross, pltpu.VMEM), pltpu.with_memory_space_constraint(var, pltpu.VMEM))
    return out, var.reshape(-1)


def solution(mesh):
    in_specs = (P("row", "col"), P("row", "col"), P(), P("col"))
    out_specs = (P("row", "col"), P("col"))
    return jax.shard_map(body, mesh=mesh, in_specs=in_specs, out_specs=out_specs, check_vma=False)
```

```python
import functools
import heapq

import jax
import jax.numpy as jnp
from jax import lax
from jax.experimental import pallas as pl
from jax.experimental.pallas import tpu as pltpu
from jax.sharding import PartitionSpec as P

MESH = pl.DeviceIdType.MESH
NX, NY, NZ = 4, 4, 8
B = 128
W = 256
NS = 4
F32, BF16 = jnp.float32, jnp.bfloat16

EARLY = (0, 1, 2, 3)
LAST = NS - 1
STEPPED = (2, 3)
LATE_D = 1
POS = (0, 3, 1, 2)
FAR = NZ // 2
SEND_POOL = 32
FIN = 2.6
Y_EXTRA = 0.4
AHEAD = 0
Y0 = -2.9
Y_SHARED = 25.0
X_WINDOW = 2
NEXT = (None, (0, 1), (1, 3), (2, 3))

LINK, LAT, CORE, CORE_LAT = 2.84, 2.1, 0.3, 1.0
T_ISSUE, T_PREP, T_TASK, T_SMALL, T_STEP, T_PART, T_BLOCK = 0.02, 0.035, 0.97, 0.05, 0.48, 0.36, 0.24
VZ_LAT, VG_LAT = 4.2, 3.0
D_ORDER = (0, 2, 3, 1)


def subs(s, h):
    first = 0 if s > 0 else 1
    return (first,) if h == FAR else (first, 1 - first)


def sgn(s):
    return "+" if s > 0 else "-"


def plan():
    program, arrivals, free, done_at = [], [], {}, {}
    clock = [0.0]
    got, seq, ends = set(), [0], {}

    def send(key, link, units=1.0):
        program.append(("send",) + key)
        clock[0] += T_ISSUE
        cost, lat = {"c": (CORE, CORE_LAT), "vz": (0.0, VZ_LAT), "vg": (0.0, VG_LAT)}.get(link, (LINK, LAT))
        start = max(clock[0], free.get(link, 0.0))
        if link == "vg":
            start = max([start] + [free.get(other, 0.0) for other in ("y+", "y-")])
        took = cost * units
        if link[0] == "y" and clock[0] > Y_SHARED:
            both = min(max(free.get("y+" if link == "y-" else "y-", 0.0) - start, 0.0), took)
            both = took if key[0] == "Y2" else both
            took = (took + both) / 2
        free[link] = start + took
        done_at[key] = ends[key] = free[link]
        seq[0] += 1
        heapq.heappush(arrivals, (free[link] + lat + (Y_EXTRA if key[0] in ("Y1", "Y2") else 0.0), seq[0], key))

    def pz(n, s, h, sub):
        send(("PZ", n, s, h, sub), "z" + sgn(s), 0.5)

    def start_slice(n, s):
        for sub in subs(s, 1):
            pz(n, s, 1, sub)

    order = {d: i for i, d in enumerate(D_ORDER)}
    held, under_way = [], {(0, 0): 2, (0, 1): 2}

    def forward_x():
        while held and len(under_way) < X_WINDOW:
            d, zz = min(held, key=lambda e: (order[e[0]], e[1]))
            if any(("own", e, f) not in got for e in D_ORDER[1:order[d]] for f in (0, 1)):
                return
            held.remove((d, zz))
            got.add(("own", d, zz))
            under_way[(d, zz)] = 2
            for s in (1, -1):
                send(("XS", d, zz, s, 1), "x" + sgn(s))

    def on(key):
        kind = key[0]
        if kind == "PZ":
            _, n, s, h, sub = key
            if h < FAR and sub in subs(s, h + 1):
                pz(n, s, h + 1, sub)
            if h == FAR:
                send(("PC", n, FAR, sub + 1), "c", 0.5)
            elif sub == subs(s, h)[1]:
                send(("PC", n, (-s * h) % NZ, 0), "c")
            for i, after in enumerate(NEXT[n + 1] if n + 1 < NS else ()):
                if (h, sub) == (after, subs(s, h)[0]):
                    pz(n + 1, s, 1, subs(s, 1)[i])
                    if s > 0 and i:
                        send(("PC", n + 1, 0, 0), "c")
        elif kind == "AR1":
            _, k, sub = key
            y = "y" + "+-"[k]
            send(("AR2", k, sub), y, 0.5)
            if not sub:
                return
            for zz in (0, 1):
                send(("AY", 1 - 2 * k, zz), y)
            for n in EARLY[:2]:
                send(("PY", n, 1 - 2 * k, 1), y)
        elif kind == "PY" and key[3] == 1:
            send(("PY", key[1], key[2], 2), "y" + sgn(key[2]), 0.5)
            if EARLY.index(key[1]) + 2 < len(EARLY):
                send(("PY", EARLY[EARLY.index(key[1]) + 2], key[2], 1), "y" + sgn(key[2]))
        elif kind in ("AY", "AR2"):
            if kind == "AR2" and not {("AR2", key[1], sub) for sub in (0, 1)} <= waited:
                return
            held.append(((-key[1]) % NY, key[2]) if kind == "AY" else (2, key[1]))
            forward_x()
        elif kind == "XS":
            _, d, zz, s, h = key
            if h == 1:
                send(("XS", d, zz, s, 2), "x" + sgn(s), 0.5)
            if h == 1:
                under_way[(d, zz)] -= 1
                if not under_way[(d, zz)]:
                    del under_way[(d, zz)]
                    forward_x()

    waited, times, came = set(), [], {}

    def receive(key):
        program.append(("recv",) + key)
        clock[0] += T_ISSUE
        waited.add(key)
        times.append((clock[0],) + key)

    def passes_on(key):
        if key[0] == "XS":
            return key[4] == 1
        if key[0] == "PY":
            return key[3] == 1
        return key[0] in ("PZ", "AR1", "AR2", "AY")

    for s in (1, -1):
        start_slice(0, s)
        for sub in (0, 1):
            send(("AR1", 0 if s > 0 else 1, sub), "y" + sgn(s), 0.5)
        send(("XS", 0, 0, s, 1), "x" + sgn(s))
    send(("PC", 0, 0, 0), "c")
    for s in (1, -1):
        send(("XS", 0, 1, s, 1), "x" + sgn(s))
        for i, after in enumerate(NEXT[1]):
            if not after:
                pz(1, s, 1, subs(s, 1)[i])
    program.append(("local",))

    jobs = {}
    arrive = {n: {} for n in range(NS)}
    for n in range(NS):
        arrive[n][0] = {("PC", n, 0, 0)}
        for s in (1, -1):
            for h in range(1, FAR + 1):
                for sub in subs(s, h):
                    rel = (-s * h) % NZ
                    arrive[n].setdefault(rel, set()).update({("PZ", n, s, h, sub), ("PC", n, rel, sub + 1 if h == FAR else 0)})
    rows = {}
    for d in range(NY):
        need = {("XS", d, zz, s, h) for zz in (0, 1) for s in (1, -1) for h in (1, 2)}
        side = 1 if d == 3 else -1
        rows[d] = need | {0: set(), 2: {("AR2", k, sub) for k in (0, 1) for sub in (0, 1)}}.get(d, {("AY", side, 0), ("AY", side, 1)})
    ready_rows = {("prepA", d) for d in range(NY) if d != LATE_D}
    for d in range(NY):
        if d != LATE_D:
            jobs[("prepA", d)] = (-1.0, rows[d], T_PREP * 8)
    blocks = {("block", 0, zz): {("AY", -1, zz)} for zz in (0, 1)}
    blocks |= {("block", (-s) % NX, zz): {("XS", LATE_D, zz, s, 1)} for zz in (0, 1) for s in (1, -1)}
    blocks |= {("block", 2, zz): {("XS", LATE_D, zz, s, 2) for s in (1, -1)} for zz in (0, 1)}
    for job, need in blocks.items():
        jobs[job] = (-1.5, need | {("prepB", n) for n in range(NS) if n not in STEPPED}, T_BLOCK)
    for n in range(NS):
        whole = n == NS - 1
        if n in STEPPED:
            steps = {("step", n, rel) for rel in range(NZ)}
            for rel in range(NZ):
                jobs[("step", n, rel)] = (n - 0.5, arrive[n][rel] | ready_rows | (set(blocks) if whole else set()), T_STEP if whole else T_PART)
        else:
            jobs[("prepB", n)] = (-2.0, set().union(*arrive[n].values()), T_PREP * 16)
        done = {}
        for d in range(NY):
            if n not in STEPPED and d == LATE_D:
                done[d] = set(blocks)
            elif n in STEPPED and (whole or d != LATE_D):
                done[d] = steps
            else:
                done[d] = {("task", d, n)}
                need = set(blocks) | steps if n in STEPPED else {("prepA", d), ("prepB", n)}
                jobs[("task", d, n)] = (n + 0.1 * POS[d] - (1 if d == 2 else 0), need, T_TASK)
        everything = set().union(*done.values())
        first = ("vpart", n)
        if n in EARLY:
            jobs[first] = (-3.5, everything | {("PY", n, s, h) for s in (1, -1) for h in (1, 2)}, 0.1)
        jobs[("y2", n)] = (-3.0, done[2], 0.0)
        for s in (1, -1):
            after = {("y2", AHEAD)} if s % NY == LATE_D and n < AHEAD and n not in STEPPED else set()
            jobs[("y0", n, s)] = (Y0, done[s % NY] | after, 0.0)
            jobs[("y1", n, s)] = (-3.0, done[s % NY] | {("Y2", n, s)} | after, T_SMALL)
        jobs[("fin", n)] = (FIN, ({first} if n in EARLY else done[0]) | {("Y1", n, s, i) for s in (1, -1) for i in (0, 1)} | {("vpart", LAST)}, T_SMALL)
    jobs[("v1",)] = (-4.0, {("vpart", n) for n in EARLY} | {("fin", n) for n in range(NS) if n not in EARLY}, 0.0)
    jobs[("v2",)] = (-4.0, {("VG",)}, 0.05)
    jobs[("vend",)] = (-4.0, {("VZ",)}, 0.05)
    while jobs or arrivals:
        if arrivals and arrivals[0][0] <= clock[0]:
            when, _, key = heapq.heappop(arrivals)
            came[key] = when
            got.add(key)
            if passes_on(key):
                receive(key)
                on(key)
            continue
        ready = [(p, j) for j, (p, need, _) in jobs.items() if need <= got]
        if ready:
            job = min(ready, key=lambda r: (r[0], str(r[1])))[1]
            for key in sorted(jobs[job][1], key=str):
                if key[0].isupper() and key not in waited:
                    receive(key)
            program.append(job)
            times.append((clock[0],) + job)
            clock[0] += jobs.pop(job)[2]
            got.add(job)
            if job[0] == "y2":
                for s in (1, -1):
                    send(("Y2", job[1], s), "y" + sgn(s), 0.5)
            elif job[0] == "y1":
                send(("Y1", job[1], job[2], 1), "y" + sgn(job[2]), 0.5)
            elif job[0] == "y0":
                send(("Y1", job[1], job[2], 0), "y" + sgn(job[2]), 0.5)
            elif job[0] == "v1":
                send(("VG",), "vg")
            elif job[0] == "v2":
                send(("VZ",), "vz")
            continue
        old = [k for k in came if k not in waited and k[0] != "Y1" and came[k] + 2.0 < clock[0]]
        if old and arrivals and arrivals[0][0] > clock[0] + 0.1:
            receive(min(old, key=lambda k: (came[k], str(k))))
            continue
        late = sorted((t, k) for k, t in done_at.items() if t + 3.0 < clock[0])
        if late and arrivals and arrivals[0][0] > clock[0] + 0.1:
            program.append(("sent",) + late[0][1])
            del done_at[late[0][1]]
            clock[0] += 0.03
            continue
        clock[0] = max(clock[0], arrivals[0][0])

    final, slots, pool, flying = [], {}, list(range(SEND_POOL)), []
    for act in program:
        key = act[1:]
        if act[0] == "send" and key[0] not in ("VZ", "VG"):
            if not pool:
                old = min(flying, key=lambda k: (ends[k], str(k)))
                final.append(("sent",) + old)
                flying.remove(old)
                pool.append(slots[old])
            slots[key] = pool.pop(0)
            flying.append(key)
        if act[0] == "sent":
            if key not in flying:
                continue
            flying.remove(key)
            pool.append(slots[key])
        final.append(act)
    for key in flying + [("VZ",), ("VG",)]:
        final.append(("sent",) + key)
    return final, slots, clock[0], free, times


def receive_slots(program):
    at = {act: i for i, act in enumerate(program)}
    keys = [act[1:] for act in program if act[0] == "send"]

    def channel(key):
        if key[0] == "PC":
            return "c", 0
        if key[0] in ("AR1", "AR2"):
            return "y", 1 - 2 * key[1]
        return {"P": "z", "X": "x", "A": "y", "Y": "y"}["Y" if key[0] == "PY" else key[0][0]], key[{"PZ": 2, "XS": 3, "AY": 1, "PY": 2, "Y2": 2, "Y1": 2}[key[0]]]

    slots, users = {}, []
    for key in keys:
        if key[0] in ("VZ", "VG"):
            users.append(None)
            slots[key] = len(users) - 1
            continue
        axis, s = channel(key)
        back = [m for m in keys if m[0] not in ("VZ", "VG") and channel(m) == (axis, -s)]
        free = None
        for i, last in enumerate(users):
            if last is None:
                continue
            if any(at[("send",) + m] > at[("recv",) + last] and at[("recv",) + m] < at[("send",) + key] for m in back):
                free = i
                break
        if free is None:
            users.append(key)
            free = len(users) - 1
        users[free] = key
        slots[key] = free
    return slots


def kernel(program, slots, sem_of, pattern_hbm, sigma, panel, diag_hbm, cross, var, diag, pattern, pbuf, sbuf, relay, a_hi, a_lo, b_hi, b_lo, part, r1, r2,
           pv, vz, vg, send_sem, recv_sem, local_sem):
    row, x = lax.axis_index("row"), lax.axis_index("col")
    z, y, c = row // (2 * NY), (row // 2) % NY, row % 2
    flip_y = 1 - 2 * c

    def at(dx=0, dy=0, dz=0, flip=False):
        core = 1 - c if flip else c
        return ((((z + dz + NZ) % NZ) * NY + (y + flip_y * dy + NY) % NY) * 2 + core, (x + dx + NX) % NX)

    halves = [pl.ds(0, B // 2), pl.ds(B // 2, B // 2)]

    def lanes(start):
        return pl.ds(pl.multiple_of(start, W), W)

    def ends(key, sender):
        kind = key[0]
        if kind == "PZ":
            _, n, s, h, sub = key
            zs = (z - s * (h - 1 if sender else h) + NZ) % NZ
            dst = pbuf.at[n, 2 * zs + c, halves[sub]]
            src = panel.at[halves[sub], pl.ds(n * W, W)] if h == 1 else dst
            return src, dst, at(dz=s)
        if kind == "PC":
            _, n, rel, part_no = key
            zs = (z + rel) % NZ
            dst = pbuf.at[n, 2 * zs + (c if sender else 1 - c)]
            if part_no:
                dst = pbuf.at[n, 2 * zs + (c if sender else 1 - c), halves[part_no - 1]]
            src = panel.at[:, pl.ds(n * W, W)] if rel == 0 else dst
            return src, dst, at(flip=True)
        if kind == "AY":
            _, s, zz = key
            src = sigma.at[:, lanes(zz * NY * W + ((y + flip_y * s + NY) % NY) * W)]
            return src, sbuf.at[(-s) % NY, 2 * x + zz], at(dy=s)
        if kind == "AR1":
            _, k, sub = key
            src = sigma.at[halves[sub], lanes(k * NY * W + ((y + 2) % NY) * W)]
            return src, relay.at[k, halves[sub]], at(dy=1 - 2 * k)
        if kind == "AR2":
            _, k, sub = key
            return relay.at[k, halves[sub]], sbuf.at[2, 2 * x + k, halves[sub]], at(dy=1 - 2 * k)
        if kind == "XS":
            _, d, zz, s, h = key
            xs = (x - s * (h - 1 if sender else h) + NX) % NX
            dst = sbuf.at[d, 2 * xs + zz]
            if h == 2:
                dst = sbuf.at[d, 2 * xs + zz, halves[(1 - s) // 2]]
            src = sigma.at[:, lanes(zz * NY * W + y * W)] if d == 0 and h == 1 else dst
            return src, dst, at(dx=s)
        if kind == "PY":
            _, n, s, h = key
            e = EARLY.index(n)
            if h == 1:
                return panel.at[:, pl.ds(n * W, W)], pv.at[e, (-s) % NY], at(dy=s)
            half = halves[(1 - s) // 2]
            return pv.at[e, (-s) % NY, half], pv.at[e, 2, half], at(dy=s)
        if kind == "Y2":
            _, n, s = key
            i = 0 if s > 0 else 1
            return part.at[n, POS[2], pl.ds(i * (B // 2), B // 2)], r1.at[i, n], at(dy=s)
        _, n, s, i = key
        half = halves[(1 - s) // 2 if i else (1 + s) // 2]
        side = 0 if s > 0 else 1
        return r1.at[side, n] if i else part.at[n, POS[s % NY], half], r2.at[0 if s > 0 else 1, n, half], at(dy=s)

    def copy(key, sender):
        src, dst, target = ends(key, sender)
        return pltpu.make_async_remote_copy(
            src_ref=src if sender else dst, dst_ref=dst, send_sem=send_sem.at[slots[key]], recv_sem=recv_sem.at[sem_of[key]],
            device_id=target, device_id_type=MESH)

    def column_sums(kind, ref=None, peer=None):
        buf, mine = (vz, z) if kind == "VZ" else (vg, me8)
        ref = buf.at[pl.ds(0, 7)] if peer is None else buf.at[mine]
        i = 0 if kind == "VZ" else 1
        return pltpu.make_async_remote_copy(
            src_ref=ref, dst_ref=ref, send_sem=send_sem.at[SEND_POOL + i], recv_sem=recv_sem.at[sem_of[(kind,)]],
            device_id=at(dz=1) if peer is None else peer, device_id_type=MESH)

    me8 = row % (2 * NY)
    barrier = pltpu.get_barrier_semaphore()
    peers = [at(dx=1), at(dx=-1), at(dy=1), at(dy=-1), at(dz=1), at(dz=-1), at(flip=True)]
    for peer in peers:
        pl.semaphore_signal(barrier, inc=1, device_id=peer, device_id_type=MESH)
    locals_ = [pltpu.make_async_copy(panel.at[:, pl.ds(n * W, W)], pbuf.at[n, 2 * z + c], local_sem.at[n]) for n in range(NS)]
    locals_ += [pltpu.make_async_copy(sigma.at[:, lanes(zz * NY * W + y * W)], sbuf.at[0, 2 * x + zz], local_sem.at[NS + zz]) for zz in (0, 1)]
    locals_ += [pltpu.make_async_copy(pattern_hbm, pattern, local_sem.at[NS + 2])]
    locals_ += [pltpu.make_async_copy(diag_hbm, diag, local_sem.at[NS + 3])]
    pl.semaphore_wait(barrier, len(peers))

    def split_a(d, zk):
        rb = (z * NY + (y + flip_y * d + NY) % NY) * 2 + c
        cb = (zk * NY + y) * 2
        for j in (0, 1):
            m = pattern[rb, cb + j].astype(F32)
            v = sbuf[d, zk, :, pl.ds(j * B, B)] * m
            hi = v.astype(BF16)
            a_hi[zk, pl.ds(POS[d] * B, B), pl.ds(j * B, B)] = hi
            a_lo[zk, pl.ds(POS[d] * B, B), pl.ds(j * B, B)] = (v - hi.astype(F32)).astype(BF16)

    def prep_a(d):
        def one(zk, carry):
            split_a(d, zk)
            return carry

        lax.fori_loop(0, NZ, one, 0)

    def split_b(n, k):
        for j in (0, 1):
            p = pbuf[n, 2 * k + j]
            hi = p.astype(BF16)
            b_hi[n, k, pl.ds(j * B, B)] = hi
            b_lo[n, k, pl.ds(j * B, B)] = (p - hi.astype(F32)).astype(BF16)

    def prep_b(n):
        def one(k, carry):
            split_b(n, k)
            return carry

        lax.fori_loop(0, NZ, one, 0)

    dot = functools.partial(jnp.dot, preferred_element_type=F32)

    def product(n, k, lo, hi):
        ah, al = a_hi[k, pl.ds(lo * B, (hi - lo) * B)], a_lo[k, pl.ds(lo * B, (hi - lo) * B)]
        return dot(ah, b_hi[n, k]) + (dot(ah, b_lo[n, k]) + dot(al, b_hi[n, k]))

    begun = set()

    def add_product(n, k, lo, hi):
        res = product(n, k, lo, hi).reshape(hi - lo, B, W)
        part[n, pl.ds(lo, hi - lo)] = part[n, pl.ds(lo, hi - lo)] + res if (n, lo) in begun else res
        begun.add((n, lo))

    def task(d, n):
        acc = jnp.zeros((B, W), F32)
        for k in range(NZ):
            acc = acc + product(n, k, POS[d], POS[d] + 1)
        part[n, POS[d]] = acc

    def step(n, rel):
        k = (z + rel) % NZ
        split_b(n, k)
        add_product(n, k, 0, NY if n == NS - 1 else NY - 1)

    def block(xr, zz):
        k = 2 * ((x + xr) % NX) + zz
        split_a(LATE_D, k)
        for n in range(NS):
            if n not in STEPPED:
                add_product(n, k, POS[LATE_D], POS[LATE_D] + 1)

    def put_var(n, prod):
        for j in (0, 1):
            vg[me8, pl.ds(2 * n + j, 1)] = prod[:, j * B:(j + 1) * B]

    for act in program:
        kind = act[0]
        if kind == "send":
            if act[1] == "VZ":
                for r in range(1, NZ):
                    column_sums("VZ", peer=at(dz=r)).start()
            elif act[1] == "VG":
                for r in range(1, 2 * NY):
                    column_sums("VG", peer=(z * 2 * NY + (me8 + r) % (2 * NY), x)).start()
            else:
                copy(act[1:], True).start()
        elif kind == "recv":
            if act[1] in ("VZ", "VG"):
                column_sums(act[1]).wait_recv()
            else:
                copy(act[1:], False).wait_recv()
        elif kind == "sent":
            if act[1] in ("VZ", "VG"):
                column_sums(act[1]).wait_send()
            else:
                copy(act[1:], True).wait_send()
        elif kind == "local":
            for cp in locals_:
                cp.start()
            for cp in locals_:
                cp.wait()
        elif kind == "prepA":
            prep_a(act[1])
        elif kind == "prepB":
            prep_b(act[1])
        elif kind == "task":
            task(act[1], act[2])
        elif kind == "step":
            step(act[1], act[2])
        elif kind == "block":
            block(act[1], act[2])
        elif kind == "y1":
            _, n, s = act
            i = 0 if s > 0 else 1
            half = pl.ds(i * (B // 2), B // 2)
            r1[i, n] = part[n, POS[s % NY], half] + r1[i, n]
        elif kind == "fin":
            n = act[1]
            out = part[n, 0] + (r2[0, n] + r2[1, n])
            cross[:, pl.ds(n * W, W)] = -out
            if n not in EARLY:
                put_var(n, jnp.sum(out * pbuf[n, 2 * z + c], axis=0, keepdims=True))
        elif kind == "vpart":
            n = act[1]
            prod = part[n, 0] * pbuf[n, 2 * z + c]
            for d in range(1, NY):
                prod = prod + part[n, POS[d]] * pv[EARLY.index(n), d]
            put_var(n, jnp.sum(prod, axis=0, keepdims=True))
        elif kind == "v2":
            total = vg[0]
            for i in range(1, 2 * NY):
                total = total + vg[i]
            vz[z] = total
        elif kind == "vend":
            total = vz[0]
            for i in range(1, NZ):
                total = total + vz[i]
            var[...] = diag[...] + total


def finish(cross, var, cross_out, var_out, sem):
    copies = [pltpu.make_async_copy(cross, cross_out, sem.at[0]), pltpu.make_async_copy(var, var_out, sem.at[1])]
    for copy in copies:
        copy.start()
    for copy in copies:
        copy.wait()


def body(sigma_anc, panel_hat, pattern, diag_inverse):
    program, slots = plan()[:2]
    sem_of = receive_slots(program)
    dma = pltpu.SemaphoreType.DMA
    vmem = pl.BlockSpec(memory_space=pltpu.VMEM)
    cross, var = pl.pallas_call(
        functools.partial(kernel, program, slots, sem_of),
        out_shape=(pltpu.VMEM((B, NS * W), F32), pltpu.VMEM((8, B), F32)),
        in_specs=[pl.BlockSpec(memory_space=pltpu.HBM)] * 4,
        out_specs=(vmem, vmem),
        scratch_shapes=[
            pltpu.VMEM((8, B), F32),
            pltpu.SMEM((NY * NZ * 2, NY * NZ * 2), jnp.int32),
            pltpu.VMEM((NS, 2 * NZ, B, W), F32),
            pltpu.VMEM((NY, NZ, B, W), F32),
            pltpu.VMEM((2, B, W), F32),
            pltpu.VMEM((NZ, NY * B, W), BF16),
            pltpu.VMEM((NZ, NY * B, W), BF16),
            pltpu.VMEM((NS, NZ, W, W), BF16),
            pltpu.VMEM((NS, NZ, W, W), BF16),
            pltpu.VMEM((NS, NY, B, W), F32),
            pltpu.VMEM((2, NS, B // 2, W), F32),
            pltpu.VMEM((2, NS, B, W), F32),
            pltpu.VMEM((len(EARLY), NY, B, W), F32),
            pltpu.VMEM((NZ, 8, B), F32),
            pltpu.VMEM((2 * NY, 8, B), F32),
            dma((SEND_POOL + 2,)),
            dma((max(sem_of.values()) + 1,)),
            dma((NS + 4,)),
        ],
        compiler_params=pltpu.CompilerParams(collective_id=0, has_side_effects=True, vmem_limit_bytes=56 * 1024 * 1024),
        name="selected_inverse",
    )(pattern, sigma_anc, panel_hat, diag_inverse.reshape(8, B))
    out, var = pl.pallas_call(
        finish,
        out_shape=(jax.ShapeDtypeStruct((B, NS * W), F32), jax.ShapeDtypeStruct((8, B), F32)),
        in_specs=[vmem, vmem],
        out_specs=(pl.BlockSpec(memory_space=pl.ANY),) * 2,
        scratch_shapes=[dma((2,))],
        name="finish",
    )(pltpu.with_memory_space_constraint(cross, pltpu.VMEM), pltpu.with_memory_space_constraint(var, pltpu.VMEM))
    return out, var.reshape(-1)


def solution(mesh):
    in_specs = (P("row", "col"), P("row", "col"), P(), P("col"))
    out_specs = (P("row", "col"), P("col"))
    return jax.shard_map(body, mesh=mesh, in_specs=in_specs, out_specs=out_specs, check_vma=False)
```
